512 devices in a mesh: rep: 4 (over z_hi), fsdp: 128 (over z_lo, y, x, core).
Axes of the slice: x: 4, y: 8, z: 8 (z_hi: 4, z_lo: 2; z = z_hi * 2 + z_lo), core: 2. Of those that a mesh axis runs over, the one named last changes fastest.
Arguments:
- hidden: bfloat16 [4, 32768, 128], P('rep', 'fsdp'), may hold values from -4 to 4
- cotangent: bfloat16 [4, 32768, 8192], P('rep', 'fsdp'), may hold values from -0.0625 to 0.0625
- master: float32 [4, 128, 8192], P('rep', 'fsdp'), may hold values from -6 to 6
- adam_m: float32 [4, 128, 8192], P('rep', 'fsdp'), may hold values from -0.3125 to 0.3125
- adam_v: float32 [4, 128, 8192], P('rep', 'fsdp'), may hold values from 0.0005 to 0.008
- anchor: float32 [128, 8192], P('fsdp'), may hold values from -6 to 6
- outer_mom: float32 [128, 8192], P('fsdp'), may hold values from -1.75 to 1.75
- next_hidden: bfloat16 [4, 4096, 128], P('rep', 'fsdp'), may hold values from -0.5 to 0.5
Outputs:
- grad_hidden: bfloat16 [4, 32768, 128], P('rep', 'fsdp')
- merged: float32 [4, 128, 8192], P('rep', 'fsdp')
- new_anchor: float32 [128, 8192], P('fsdp')
- new_momentum: float32 [128, 8192], P('fsdp')
- next_out: bfloat16 [4, 4096, 8192], P('rep', 'fsdp')
The draws below stay inside these ranges and needn't reach their ends.
All inputs are finite; a program needn't handle non-finite values.
Results may differ from the reference program's by a relative error of at most 0.018.
Values may be sent and summed in bfloat16 or wider, within the bound.
A program may use at most 64 MiB of HBM per device.

```python
import math
import jax
import jax.numpy as jnp
from jax import lax

D = 8192
R = 128
TOKENS = 32768
NEXT = 4096
N_REP = 4


def spiked(values, rng, source, target, blocks, factor):
    owner, partner = [(jnp.arange(values.shape[position]) // (values.shape[position] // blocks)).reshape([-1 if axis == position else 1 for axis in range(values.ndim)]) for position in (source, target)]
    chosen = jax.random.permutation(rng, blocks)[partner]
    strong = (owner == chosen) | (owner == (partner + blocks // 2) % blocks)
    return jnp.where(strong, factor * values, values)


def steps_of(own_key, shape, shards, least, top_value):
    level = 1.0
    for dim, blocks in shards:
        heights = jax.random.uniform(jax.random.fold_in(jax.random.fold_in(own_key, 6), dim), (blocks,), jnp.float32, least / len(shards), top_value / len(shards))
        level = level * jnp.repeat(jnp.exp(heights), shape[dim] // blocks).reshape((-1,) + (1,) * (len(shape) - 1 - dim))
    return level


def normal_values(own_key, shape, scale, bound, pieces=(), held_as=jnp.bfloat16):
    drawn = scale * jax.random.normal(own_key, shape, jnp.float32)
    if pieces:
        drawn = drawn * steps_of(own_key, shape, pieces, -0.22, 0.18)
    return jnp.clip(drawn, -bound, bound).astype(held_as)


def gaussian_with(key, shape, scale, reach, split, heavy, kind=jnp.bfloat16):
    drawn = scale * jax.random.normal(key, shape, jnp.float32)
    if split:
        drawn = drawn * steps_of(key, shape, split, -0.22, 0.18)
    return jnp.clip(spiked(drawn, jax.random.fold_in(key, 3), *heavy), -reach, reach).astype(kind)


def setup_inputs(seed: int = 0) -> dict:
    key_of = jax.random.split(jax.random.key(seed), 9)
    return {
        "hidden": gaussian_with(key_of[0], (N_REP, TOKENS, R), (2.0 * R ** -0.5), 4.0, ((0, 4), (1, 128)), (1, 2, 128, 5.5)),
        "cotangent": normal_values(key_of[1], (N_REP, TOKENS, D), (D ** -0.5), 0.0625, ((0, 4), (1, 128))),
        "master": normal_values(key_of[2], (N_REP, R, D), 1.0, 6.0, ((0, 4), (1, 128)), jnp.float32),
        "adam_m": normal_values(key_of[3], (N_REP, R, D), 0.05, 0.3125, ((0, 4), (1, 128)), jnp.float32),
        "adam_v": jnp.clip(jnp.exp(math.log(0.008) - 2.7725887 * jax.random.uniform(key_of[4], (N_REP, R, D), jnp.float32) ** steps_of(key_of[4], (N_REP, R, D), ((0, 4), (1, 128)), -0.2, 0.2)), 0.0005, 0.008),
        "anchor": normal_values(key_of[5], (R, D), 1.0, 6.0, ((0, 128),), jnp.float32),
        "outer_mom": normal_values(key_of[6], (R, D), 0.3, 1.75, ((0, 128),), jnp.float32),
        "next_hidden": normal_values(key_of[7], (N_REP, NEXT, R), (R ** -0.5), 0.5, ((0, 4), (1, 128))),
    }


BETA_ONE = 0.9
BETA_TWO = 0.95
INNER_LR = 0.3
DECAY = 0.1
EPS = 1e-08
OUTER_LR = 0.7
MOMENTUM = 0.9
ALPHA = 0.5
STEP = 100

def hadamard_table():
    index = jnp.arange(128, dtype=jnp.int32)
    count = jnp.zeros((128, 128), jnp.int32)
    for bit in range(7):
        left = jnp.bitwise_and(jnp.right_shift(index, bit), 1)
        count = count + left[:, None] * left[None, :]
    return (1 - 2 * (count % 2)).astype(jnp.float32)

def sign_vector(offset, width):
    index = offset + jnp.arange(width, dtype=jnp.int32)
    return (1 - 2 * (index * 97 % 251 % 2)).astype(jnp.float32)

def block_rotate(values, table):
    rows, width = values.shape
    blocks = values.reshape(rows, width // 128, 128)
    out = jnp.einsum('rbk,kj->rbj', blocks, table, precision=lax.Precision.HIGHEST)
    return out.reshape(rows, width) * (1.0 / math.sqrt(128.0))

def reference(hidden, cotangent, master, adam_m, adam_v, anchor, outer_mom, next_hidden):
    table = hadamard_table()
    signs = sign_vector(0, D)
    corr_one = 1.0 - BETA_ONE ** STEP
    corr_two = 1.0 - BETA_TWO ** STEP
    total = jnp.zeros(anchor.shape, jnp.float32)
    grads_out = []
    inners = []
    for index in range(N_REP):
        weights16 = master[index].astype(jnp.bfloat16)
        grads_out.append(jnp.dot(cotangent[index], weights16.T, preferred_element_type=jnp.float32).astype(jnp.bfloat16))
        gradient = jnp.dot(hidden[index].T, cotangent[index], preferred_element_type=jnp.float32)
        first = BETA_ONE * adam_m[index] + (1.0 - BETA_ONE) * gradient
        second = BETA_TWO * adam_v[index] + (1.0 - BETA_TWO) * gradient * gradient
        update = first / corr_one / (jnp.sqrt(second / corr_two) + EPS) + DECAY * master[index]
        inner = master[index] - INNER_LR * update
        inners.append(inner)
        rotated = block_rotate((anchor - inner) * signs[None, :], table).astype(jnp.bfloat16)
        total = total + rotated.astype(jnp.float32)
    mean_delta = block_rotate(total, table) * signs[None, :] / N_REP
    new_momentum = MOMENTUM * outer_mom + mean_delta
    new_anchor = anchor - OUTER_LR * (MOMENTUM * new_momentum + mean_delta)
    merged_list = []
    outs = []
    for index in range(N_REP):
        merged = ALPHA * inners[index] + (1.0 - ALPHA) * new_anchor
        merged_list.append(merged)
        outs.append(jnp.dot(next_hidden[index], merged.astype(jnp.bfloat16), preferred_element_type=jnp.float32).astype(jnp.bfloat16))
    return (jnp.stack(grads_out), jnp.stack(merged_list), new_anchor, new_momentum, jnp.stack(outs))
```

```python
import functools
import math

import jax
import jax.numpy as jnp
from jax import lax
from jax.experimental import pallas as pl
from jax.experimental.pallas import tpu as pltpu
from jax.sharding import PartitionSpec as P

BETA_ONE = 0.9
BETA_TWO = 0.95
INNER_LR = 0.3
DECAY = 0.1
EPS = 1e-08
OUTER_LR = 0.7
MOMENTUM = 0.9
ALPHA = 0.5
STEP = 100

BF16 = jnp.bfloat16
F32 = jnp.float32


def row_table():
    p = lax.broadcasted_iota(jnp.int32, (128, 128), 0)
    f = lax.broadcasted_iota(jnp.int32, (128, 128), 1)
    x = lax.shift_right_logical(p, 5)
    y = lax.bitwise_and(lax.shift_right_logical(p, 2), 7)
    z = lax.bitwise_and(lax.shift_right_logical(p, 1), 1)
    c = lax.bitwise_and(p, 1)
    return jnp.where(f == z * 64 + y * 8 + x * 2 + c, 1.0, 0.0).astype(BF16)


def hadamard_table():
    i = lax.broadcasted_iota(jnp.int32, (128, 128), 0)
    j = lax.broadcasted_iota(jnp.int32, (128, 128), 1)
    bits = lax.bitwise_and(i, j)
    bits = lax.bitwise_xor(bits, lax.shift_right_logical(bits, 4))
    bits = lax.bitwise_xor(bits, lax.shift_right_logical(bits, 2))
    bits = lax.bitwise_xor(bits, lax.shift_right_logical(bits, 1))
    return (1 - 2 * lax.bitwise_and(bits, 1)).astype(F32)


def sign_table():
    j = lax.broadcasted_iota(jnp.int32, (64, 128), 0) * 128 + lax.broadcasted_iota(
        jnp.int32, (64, 128), 1
    )
    return (1 - 2 * lax.rem(lax.rem(97 * j, 251), 2)).astype(F32)


def rotate(values, table):
    out = jnp.dot(
        values, table, precision=lax.Precision.HIGHEST, preferred_element_type=F32
    )
    return out * (1.0 / math.sqrt(128.0))


def copy_to(src, dst, send_sem, recv_sem, device):
    return pltpu.make_async_remote_copy(
        src_ref=src,
        dst_ref=dst,
        send_sem=send_sem,
        recv_sem=recv_sem,
        device_id=device,
        device_id_type=pl.DeviceIdType.MESH,
    )


def aligned(index, size):
    return pl.ds(pl.multiple_of(index * size, size), size)


def kernel(
    hidden, cot, master, adam_m, adam_v, anchor, outer_mom, next_hidden,
    grad_hidden, merged_out, anchor_out, mom_out, next_out,
    cotv, part, core_send, core_recv, x_send, x_recv, rows, y_send, y_recv,
    zc_sum, zc_send, zc_recv, grad, rot, row16, ag_y, ag_rows, weights,
    cot_sem, core_ss, core_rs, x_ss, x_rs, y_ss, y_rs, zc_ss, zc_rs,
    rep_ss, rep_rs, agz_ss, agz_rs, agy_ss, agy_rs, agx_ss, agx_rs, agc_ss, agc_rs,
):
    rep = lax.axis_index("rep")
    me = lax.axis_index("fsdp")
    z = lax.div(me, 64)
    y = lax.rem(lax.div(me, 8), 8)
    x = lax.rem(lax.div(me, 2), 4)
    c = lax.rem(me, 2)

    def at(zz, yy, xx, cc):
        return {"fsdp": zz * 64 + yy * 8 + xx * 2 + cc}

    pairs = ((0, 1), (1, 0), (1, 1))

    def flip(index):
        dz, dc = pairs[index]
        return (1 - z if dz else z), (1 - c if dc else c)

    partner = at(z, y, x, 1 - c)
    x_peers = [lax.rem(x + d, 4) for d in range(1, 4)]
    x_from = [lax.rem(x + 4 - d, 4) for d in range(1, 4)]
    y_peers = [lax.rem(y + d, 8) for d in range(1, 8)]

    barrier = pltpu.get_barrier_semaphore()
    peers = [at(flip(i)[0], y, x, flip(i)[1]) for i in range(3)]
    peers += [at(z, y, xx, c) for xx in x_peers]
    peers += [at(z, yy, x, c) for yy in y_peers]
    peers += [{"rep": lax.rem(rep + d, 4)} for d in range(1, 4)]
    for peer in peers:
        pl.semaphore_signal(
            barrier, inc=1, device_id=peer, device_id_type=pl.DeviceIdType.MESH
        )

    halves = (1 - c, c)
    loads = []
    for h in range(2):
        for q in range(4):
            start = pl.multiple_of(halves[h] * 4096 + q * 1024, 1024)
            load = pltpu.make_async_copy(
                cot.at[:, pl.ds(start, 1024)], cotv.at[h, q], cot_sem.at[h * 4 + q]
            )
            load.start()
            loads.append(load)

    row16[0] = master[...].astype(BF16)
    order = row_table()
    turned = lax.dot_general(
        order, hidden[...], (((1,), (1,)), ((), ())), preferred_element_type=F32
    ).astype(BF16)

    pl.semaphore_wait(barrier, len(peers))
    sends = []

    def start(copy):
        copy.start()
        sends.append(copy)
        return copy

    def gather_zc(k):
        for i in range(3):
            zz, cc = flip(i)
            start(
                copy_to(
                    row16.at[k, aligned(cc, 32)],
                    ag_y.at[k, y, aligned(z * 2 + c, 32)],
                    agz_ss.at[k, i], agz_rs.at[k, i], at(zz, y, x, cc),
                )
            )
        ag_y[k, y, aligned(z * 2 + c, 32), :] = row16[k, aligned(c, 32), :]
        return sends[-3:]

    def gather_y(k, before):
        for copy in before:
            copy.wait_recv()
        for d in range(7):
            start(
                copy_to(
                    ag_y.at[k, y], ag_y.at[k, y],
                    agy_ss.at[k, d], agy_rs.at[k, d], at(z, y_peers[d], x, c),
                )
            )
        return sends[-7:]

    def gather_x(k, before):
        for copy in before:
            copy.wait_recv()
        ag_rows[k] = ag_y[k].reshape(1024, 128).astype(F32)
        mine = aligned(x, 32)
        for b in range(32):
            block = ag_rows[k, pl.ds(b, 32, stride=32), :]
            weights[k, 1, mine, b * 128 : (b + 1) * 128] = block.astype(BF16)
        copies = []
        for d in range(3):
            copies.append(
                start(
                    copy_to(
                        weights.at[k, 1, mine], weights.at[k, 1, mine],
                        agx_ss.at[k, d], agx_rs.at[k, d], at(z, y, x_peers[d], c),
                    )
                )
            )
        cores = [
            start(
                copy_to(
                    weights.at[k, 1, mine], weights.at[k, 0, mine],
                    agc_ss.at[k, 0], agc_rs.at[k, 0], partner,
                )
            )
        ]
        return copies, cores

    def gather_core(k, copies, cores):
        for d in range(3):
            copies[d].wait_recv()
            block = aligned(x_from[d], 32)
            cores.append(
                start(
                    copy_to(
                        weights.at[k, 1, block], weights.at[k, 0, block],
                        agc_ss.at[k, d + 1], agc_rs.at[k, d + 1], partner,
                    )
                )
            )
        return cores

    zc_copies = gather_zc(0)

    core_copies = []
    for q in range(4):
        loads[q].wait()
        core_send[q] = jnp.dot(
            turned, cotv[0, q], preferred_element_type=F32
        ).astype(BF16)
        core_copies.append(
            start(
                copy_to(
                    core_send.at[q], core_recv.at[q], core_ss.at[q], core_rs.at[q], partner
                )
            )
        )
    y_copies = gather_y(0, zc_copies)
    for q in range(4):
        loads[4 + q].wait()
        part[q] = jnp.dot(turned, cotv[1, q], preferred_element_type=F32)

    x_copies = []
    for q in range(4):
        core_copies[q].wait_recv()
        both = part[q] + core_recv[q].astype(F32)
        part[q] = both
        x_send[q] = both.astype(BF16)
        for d in range(3):
            x_copies.append(
                start(
                    copy_to(
                        x_send.at[q, aligned(x_peers[d], 32)], x_recv.at[q, d],
                        x_ss.at[q, d], x_rs.at[q, d], at(z, y, x_peers[d], c),
                    )
                )
            )
    for q in range(4):
        for d in range(3):
            x_copies[3 * q + d].wait_recv()
        total = part[q, aligned(x, 32), :]
        for d in range(3):
            total = total + x_recv[q, d].astype(F32)
        for b in range(8):
            rows[pl.ds(q * 8 + b, 32, stride=32), :] = total[:, b * 128 : (b + 1) * 128]

    y_send[...] = rows[...].astype(BF16)
    rs_y = []
    for d in range(7):
        rs_y.append(
            start(
                copy_to(
                    y_send.at[aligned(y_peers[d], 128)], y_recv.at[d],
                    y_ss.at[d], y_rs.at[d], at(z, y_peers[d], x, c),
                )
            )
        )
    x_gathers, c_gathers = gather_x(0, y_copies)

    total = rows[aligned(y, 128), :]
    for d in range(7):
        rs_y[d].wait_recv()
        total = total + y_recv[d].astype(F32)
    zc_sum[...] = total
    zc_send[...] = total.astype(BF16)
    rs_zc = []
    for i in range(3):
        zz, cc = flip(i)
        rs_zc.append(
            start(
                copy_to(
                    zc_send.at[aligned(zz * 2 + cc, 32)], zc_recv.at[i],
                    zc_ss.at[i], zc_rs.at[i], at(zz, y, x, cc),
                )
            )
        )
    table = hadamard_table()
    signs = sign_table()
    for copy in rs_zc:
        copy.wait_recv()
    grad[aligned(c, 32), :] = zc_sum[aligned(z * 2 + c, 32), :] + zc_recv[1].astype(F32)
    grad[aligned(1 - c, 32), :] = zc_recv[0].astype(F32) + zc_recv[2].astype(F32)

    gradient = grad[...]
    first = BETA_ONE * adam_m[...] + (1.0 - BETA_ONE) * gradient
    second = BETA_TWO * adam_v[...] + (1.0 - BETA_TWO) * gradient * gradient
    corr_one = 1.0 - BETA_ONE**STEP
    corr_two = 1.0 - BETA_TWO**STEP
    update = first / corr_one / (jnp.sqrt(second / corr_two) + EPS) + DECAY * master[...]
    inner = master[...] - INNER_LR * update
    rot[rep] = rotate((anchor[...] - inner) * signs, table).astype(BF16)
    rep_copies = []
    for d in range(3):
        rep_copies.append(
            start(
                copy_to(
                    rot.at[rep], rot.at[rep], rep_ss.at[d], rep_rs.at[d],
                    {"rep": lax.rem(rep + d + 1, 4)},
                )
            )
        )
    c_gathers = gather_core(0, x_gathers, c_gathers)
    for copy in rep_copies:
        copy.wait_recv()
    total = rot[0].astype(F32)
    for r in range(1, 4):
        total = total + rot[r].astype(F32)
    mean_delta = rotate(total, table) * signs * 0.25
    new_momentum = MOMENTUM * outer_mom[...] + mean_delta
    new_anchor = anchor[...] - OUTER_LR * (MOMENTUM * new_momentum + mean_delta)
    merged = ALPHA * inner + (1.0 - ALPHA) * new_anchor
    row16[1] = merged.astype(BF16)
    zc_copies = gather_zc(1)
    mom_out[...] = new_momentum
    anchor_out[...] = new_anchor
    merged_out[...] = merged
    y_copies = gather_y(1, zc_copies)

    for copy in c_gathers:
        copy.wait_recv()
    products = jnp.zeros((256, 128), F32)
    for h in range(2):
        for q in range(4):
            products = products + lax.dot_general(
                cotv[h, q], weights[0, h, :, q * 1024 : (q + 1) * 1024],
                (((1,), (1,)), ((), ())), preferred_element_type=F32,
            )
    grad_hidden[...] = jnp.dot(
        products.astype(BF16), order, preferred_element_type=F32
    ).astype(BF16)
    ahead = lax.dot_general(
        next_hidden[...], order, (((1,), (1,)), ((), ())), preferred_element_type=F32
    ).astype(BF16)

    x_gathers, c_gathers = gather_x(1, y_copies)
    c_gathers = gather_core(1, x_gathers, c_gathers)
    for q in range(4):
        start_col = pl.multiple_of(c * 4096 + q * 1024, 1024)
        next_out[:, pl.ds(start_col, 1024)] = jnp.dot(
            ahead, weights[1, 1, :, q * 1024 : (q + 1) * 1024], preferred_element_type=F32
        ).astype(BF16)
    for copy in c_gathers:
        copy.wait_recv()
    for q in range(4):
        start_col = pl.multiple_of((1 - c) * 4096 + q * 1024, 1024)
        next_out[:, pl.ds(start_col, 1024)] = jnp.dot(
            ahead, weights[1, 0, :, q * 1024 : (q + 1) * 1024], preferred_element_type=F32
        ).astype(BF16)
    for copy in sends:
        copy.wait_send()


def shards(hidden, cotangent, master, adam_m, adam_v, anchor, outer_mom, next_hidden):
    vmem = pl.BlockSpec(memory_space=pltpu.VMEM)
    dma = pltpu.SemaphoreType.DMA
    row = lambda a: a.reshape(64, 128)
    outs = pl.pallas_call(
        kernel,
        out_shape=(
            jax.ShapeDtypeStruct((256, 128), BF16),
            jax.ShapeDtypeStruct((64, 128), F32),
            jax.ShapeDtypeStruct((64, 128), F32),
            jax.ShapeDtypeStruct((64, 128), F32),
            jax.ShapeDtypeStruct((32, 8192), BF16),
        ),
        in_specs=[vmem, pl.BlockSpec(memory_space=pl.ANY)] + [vmem] * 6,
        out_specs=(vmem,) * 5,
        scratch_shapes=[
            pltpu.VMEM((2, 4, 256, 1024), BF16),
            pltpu.VMEM((4, 128, 1024), F32),
            pltpu.VMEM((4, 128, 1024), BF16),
            pltpu.VMEM((4, 128, 1024), BF16),
            pltpu.VMEM((4, 128, 1024), BF16),
            pltpu.VMEM((4, 3, 32, 1024), BF16),
            pltpu.VMEM((1024, 128), F32),
            pltpu.VMEM((1024, 128), BF16),
            pltpu.VMEM((7, 128, 128), BF16),
            pltpu.VMEM((128, 128), F32),
            pltpu.VMEM((128, 128), BF16),
            pltpu.VMEM((3, 32, 128), BF16),
            pltpu.VMEM((64, 128), F32),
            pltpu.VMEM((4, 64, 128), BF16),
            pltpu.VMEM((2, 64, 128), BF16),
            pltpu.VMEM((2, 8, 128, 128), BF16),
            pltpu.VMEM((2, 1024, 128), F32),
            pltpu.VMEM((2, 2, 128, 4096), BF16),
            dma((8,)),
            dma((4,)), dma((4,)), dma((4, 3)), dma((4, 3)), dma((7,)), dma((7,)),
            dma((3,)), dma((3,)), dma((3,)), dma((3,)), dma((2, 3)), dma((2, 3)),
            dma((2, 7)), dma((2, 7)), dma((2, 3)), dma((2, 3)), dma((2, 4)), dma((2, 4)),
        ],
        compiler_params=pltpu.CompilerParams(
            collective_id=0, has_side_effects=True, vmem_limit_bytes=48 * 1024 * 1024
        ),
        name="sync",
    )(
        hidden[0], cotangent[0], row(master), row(adam_m), row(adam_v),
        row(anchor), row(outer_mom), next_hidden[0],
    )
    grad_hidden, merged, new_anchor, new_momentum, next_out = outs
    return (
        grad_hidden[None],
        merged.reshape(1, 1, 8192),
        new_anchor.reshape(1, 8192),
        new_momentum.reshape(1, 8192),
        next_out[None],
    )


def solution(mesh):
    in_specs = (
        P("rep", "fsdp", None),
        P("rep", "fsdp", None),
        P("rep", "fsdp", None),
        P("rep", "fsdp", None),
        P("rep", "fsdp", None),
        P("fsdp", None),
        P("fsdp", None),
        P("rep", "fsdp", None),
    )
    out_specs = (
        P("rep", "fsdp", None),
        P("rep", "fsdp", None),
        P("fsdp", None),
        P("fsdp", None),
        P("rep", "fsdp", None),
    )
    return jax.shard_map(shards, mesh=mesh, in_specs=in_specs, out_specs=out_specs, check_vma=False)
```

```python
import math

import jax
import jax.numpy as jnp
from jax import lax
from jax.experimental import pallas as pl
from jax.experimental.pallas import tpu as pltpu
from jax.sharding import PartitionSpec as P

BETA_ONE = 0.9
BETA_TWO = 0.95
INNER_LR = 0.3
DECAY = 0.1
EPS = 1e-08
OUTER_LR = 0.7
MOMENTUM = 0.9
ALPHA = 0.5
STEP = 100

BF16 = jnp.bfloat16
F32 = jnp.float32
VMEM_BYTES = 62 * 1024 * 1024
CHUNKS = 4
PARTS = 2
WIDE = 1024 // PARTS


def row_table():
    p = lax.broadcasted_iota(jnp.int32, (128, 128), 0)
    f = lax.broadcasted_iota(jnp.int32, (128, 128), 1)
    y = lax.shift_right_logical(p, 4)
    z = lax.bitwise_and(lax.shift_right_logical(p, 3), 1)
    return jnp.where(f == z * 64 + y * 8 + lax.bitwise_and(p, 7), 1.0, 0.0).astype(BF16)


def hadamard_table():
    i = lax.broadcasted_iota(jnp.int32, (128, 128), 0)
    j = lax.broadcasted_iota(jnp.int32, (128, 128), 1)
    bits = lax.bitwise_and(i, j)
    bits = lax.bitwise_xor(bits, lax.shift_right_logical(bits, 4))
    bits = lax.bitwise_xor(bits, lax.shift_right_logical(bits, 2))
    bits = lax.bitwise_xor(bits, lax.shift_right_logical(bits, 1))
    return (1 - 2 * lax.bitwise_and(bits, 1)).astype(F32)


def sign_table():
    j = lax.broadcasted_iota(jnp.int32, (64, 128), 0) * 128 + lax.broadcasted_iota(
        jnp.int32, (64, 128), 1
    )
    return (1 - 2 * lax.rem(lax.rem(97 * j, 251), 2)).astype(F32)


def rotate(values, table):
    out = jnp.dot(
        values, table, precision=lax.Precision.HIGHEST, preferred_element_type=F32
    )
    return out * (1.0 / math.sqrt(128.0))


def copy_to(src, dst, send_sem, recv_sem, device):
    return pltpu.make_async_remote_copy(
        src_ref=src,
        dst_ref=dst,
        send_sem=send_sem,
        recv_sem=recv_sem,
        device_id=device,
        device_id_type=pl.DeviceIdType.MESH,
    )


def aligned(index, size):
    return pl.ds(pl.multiple_of(index * size, size), size)


def kernel(
    hidden_in, cot, master_in, adam_m_in, adam_v_in, anchor_in, outer_mom_in, next_in,
    grad_hidden_out, merged_out, anchor_out, mom_out, next_out,
    grad_hidden, results, hidden, state, next_all, cotv, core_send, core_recv,
    part, x_send, x_recv, x_sum, y_send, y_recv, line_send, line_recv, grad, rot,
    row, ag_in, gathered, weights, ahead_send, ahead_out,
    out_sem, next_sem, in_sem, state_sem, cot_sem, nh_ss, nh_rs, core_ss, core_rs,
    x_ss, x_rs, y_ss, y_rs, line_ss, line_rs, rep_ss, rep_rs, ag_ss, ag_rs,
    agy_ss, agy_rs, agx_ss, agx_rs, agc_ss, agc_rs, last_ss, last_rs,
):
    rep = lax.axis_index("rep")
    me = lax.axis_index("fsdp")
    z = lax.div(me, 64)
    y = lax.rem(lax.div(me, 8), 8)
    x = lax.rem(lax.div(me, 2), 4)
    c = lax.rem(me, 2)

    def at(zz, yy, xx, cc):
        return {"fsdp": zz * 64 + yy * 8 + xx * 2 + cc}

    group = []
    for dz in range(2):
        for dx in range(4):
            for dc in range(2):
                if dz or dx or dc:
                    group.append(
                        (1 - z if dz else z, lax.rem(x + dx, 4), 1 - c if dc else c)
                    )
    plane = group[:7]
    partner = at(z, y, x, 1 - c)
    x_peers = [lax.rem(x + d, 4) for d in range(1, 4)]
    x_from = [lax.rem(x + 4 - d, 4) for d in range(1, 4)]
    y_peers = [lax.rem(y + d, 8) for d in range(1, 8)]

    barrier = pltpu.get_barrier_semaphore()
    peers = [at(zz, y, xx, cc) for zz, xx, cc in group]
    peers += [at(z, yy, x, c) for yy in y_peers]
    peers += [{"rep": lax.rem(rep + d, 4)} for d in range(1, 4)]
    for peer in peers:
        pl.semaphore_signal(
            barrier, inc=1, device_id=peer, device_id_type=pl.DeviceIdType.MESH
        )

    sends = []

    def start(copy):
        copy.start()
        sends.append(copy)
        return copy

    halves = (1 - c, c)
    seat = aligned(x * 2 + c, 32)
    loads = [
        pltpu.make_async_copy(hidden_in, hidden, in_sem.at[0]),
        pltpu.make_async_copy(master_in, state.at[0], in_sem.at[1]),
        pltpu.make_async_copy(next_in, next_all.at[seat], in_sem.at[2]),
    ]
    for load in loads:
        load.start()
    cot_loads = {}
    for h in range(2):
        for j in range(CHUNKS):
            for s in range(4):
                begin = pl.multiple_of(halves[h] * 4096 + s * 1024 + j * 256, 256)
                load = pltpu.make_async_copy(
                    cot.at[:, pl.ds(begin, 256)],
                    cotv.at[h, j, :, pl.ds(s * 256, 256)],
                    cot_sem.at[h, j, s],
                )
                load.start()
                cot_loads[h, j, s] = load
    late_loads = [
        pltpu.make_async_copy(source, state.at[i + 1], state_sem.at[i])
        for i, source in enumerate((adam_m_in, adam_v_in, anchor_in, outer_mom_in))
    ]
    for load in late_loads:
        load.start()
    master, adam_m, adam_v, anchor, outer_mom = (state.at[i] for i in range(5))

    order = row_table()
    loads[0].wait()
    turned = lax.dot_general(
        order, hidden[...], (((1,), (1,)), ((), ())), preferred_element_type=F32
    ).astype(BF16)

    def gather_lines(k):
        copies = []
        for i, (zz, xx, cc) in enumerate(group):
            copies.append(
                start(
                    copy_to(
                        row.at[k, aligned(cc * 4 + xx, 8)],
                        ag_in.at[k, aligned(z * 8 + x * 2 + c, 8)],
                        ag_ss.at[k, i], ag_rs.at[k, i], at(zz, y, xx, cc),
                    )
                )
            )
        ag_in[k, aligned(z * 8 + x * 2 + c, 8), :] = row[k, aligned(c * 4 + x, 8), :]
        return copies

    def gather_y(k, before, parts):
        for copy in before:
            copy.wait_recv()
        mine = aligned(y, 16)
        for b in range(8):
            block = ag_in[k, pl.ds(b, 16, stride=8), :]
            gathered[k, mine, b * 128 : (b + 1) * 128] = block.astype(BF16)
        copies = []
        for q in range(parts):
            cols = pl.ds(q * (1024 // parts), 1024 // parts)
            for d in range(7):
                copies.append(
                    start(
                        copy_to(
                            gathered.at[k, mine, cols], gathered.at[k, mine, cols],
                            agy_ss.at[k, q, d], agy_rs.at[k, q, d], at(z, y_peers[d], x, c),
                        )
                    )
                )
        return copies

    core_copies = []
    for j in range(CHUNKS):
        for s in range(4):
            cot_loads[0, j, s].wait()
        core_send[j] = jnp.dot(turned, cotv[0, j], preferred_element_type=F32).astype(BF16)
        if j == 0:
            pl.semaphore_wait(barrier, len(peers))
        core_copies.append(
            start(
                copy_to(
                    core_send.at[j], core_recv.at[j], core_ss.at[j], core_rs.at[j], partner
                )
            )
        )
    x_copies = []
    for j in range(CHUNKS):
        for s in range(4):
            cot_loads[1, j, s].wait()
        own = jnp.dot(turned, cotv[1, j], preferred_element_type=F32)
        core_copies[j].wait_recv()
        both = own + core_recv[j].astype(F32)
        part[j] = both
        x_send[j] = both.astype(BF16)
        for d in range(3):
            x_copies.append(
                start(
                    copy_to(
                        x_send.at[j, :, aligned(x_peers[d], 256)], x_recv.at[j, d],
                        x_ss.at[j, d], x_rs.at[j, d], at(z, y, x_peers[d], c),
                    )
                )
            )

    loads[1].wait()
    row[0] = master[...].astype(BF16).astype(F32)
    line_copies = gather_lines(0)
    loads[2].wait()
    nh_copies = []
    for i, (zz, xx, cc) in enumerate(plane):
        nh_copies.append(
            start(
                copy_to(
                    next_all.at[seat], next_all.at[seat],
                    nh_ss.at[i], nh_rs.at[i], at(zz, y, xx, cc),
                )
            )
        )
    agy_copies = gather_y(0, line_copies, 1)

    rs_y = []
    for j in range(CHUNKS):
        total = part[j, :, aligned(x, 256)]
        for d in range(3):
            x_copies[3 * j + d].wait_recv()
            total = total + x_recv[j, d].astype(F32)
        x_sum[j] = total
        y_send[j] = total.astype(BF16)
        for d in range(7):
            rs_y.append(
                start(
                    copy_to(
                        y_send.at[j, aligned(y_peers[d], 16)], y_recv.at[j, d],
                        y_ss.at[j, d], y_rs.at[j, d], at(z, y_peers[d], x, c),
                    )
                )
            )

    for copy in agy_copies:
        copy.wait_recv()
    agx_copies, agc_copies = [], []
    for d in range(3):
        agx_copies.append(
            start(
                copy_to(
                    gathered.at[0], weights.at[1, x],
                    agx_ss.at[d], agx_rs.at[d], at(z, y, x_peers[d], c),
                )
            )
        )
    agc_copies.append(
        start(
            copy_to(gathered.at[0], weights.at[0, x], agc_ss.at[0], agc_rs.at[0], partner)
        )
    )
    weights[1, x] = gathered[0]

    for j in range(CHUNKS):
        total = x_sum[j, aligned(y, 16), :]
        for d in range(7):
            rs_y[7 * j + d].wait_recv()
            total = total + y_recv[j, d].astype(F32)
        for b in range(2):
            line_send[pl.ds(2 * j + b, 16, stride=8), :] = total[:, b * 128 : (b + 1) * 128]
    rs_lines = []
    mine = aligned(z * 8 + x * 2 + c, 8)
    for i, (zz, xx, cc) in enumerate(group):
        rs_lines.append(
            start(
                copy_to(
                    line_send.at[aligned(zz * 8 + xx * 2 + cc, 8)], line_recv.at[mine],
                    line_ss.at[i], line_rs.at[i], at(zz, y, xx, cc),
                )
            )
        )
    line_recv[mine, :] = line_send[mine, :]
    table = hadamard_table()
    signs = sign_table()
    for load in late_loads:
        load.wait()
    for copy in rs_lines:
        copy.wait_recv()
    for cc in range(2):
        for xx in range(4):
            low, high = (xx * 2 + cc) * 8, (8 + xx * 2 + cc) * 8
            grad[(cc * 4 + xx) * 8 : (cc * 4 + xx + 1) * 8, :] = (
                line_recv[low : low + 8, :] + line_recv[high : high + 8, :]
            )

    gradient = grad[...]
    first = BETA_ONE * adam_m[...] + (1.0 - BETA_ONE) * gradient
    second = BETA_TWO * adam_v[...] + (1.0 - BETA_TWO) * gradient * gradient
    corr_one = 1.0 - BETA_ONE**STEP
    corr_two = 1.0 - BETA_TWO**STEP
    update = first / corr_one / (jnp.sqrt(second / corr_two) + EPS) + DECAY * master[...]
    inner = master[...] - INNER_LR * update
    rot[rep] = rotate((anchor[...] - inner) * signs, table).astype(BF16)
    rep_copies = []
    for d in range(3):
        rep_copies.append(
            start(
                copy_to(
                    rot.at[rep], rot.at[rep], rep_ss.at[d], rep_rs.at[d],
                    {"rep": lax.rem(rep + d + 1, 4)},
                )
            )
        )
    for copy in nh_copies:
        copy.wait_recv()
    ahead = lax.dot_general(
        next_all[...], order, (((1,), (1,)), ((), ())), preferred_element_type=F32
    ).astype(BF16)
    for copy in rep_copies:
        copy.wait_recv()
    total = rot[0].astype(F32)
    for r in range(1, 4):
        total = total + rot[r].astype(F32)
    mean_delta = rotate(total, table) * signs * 0.25
    new_momentum = MOMENTUM * outer_mom[...] + mean_delta
    new_anchor = anchor[...] - OUTER_LR * (MOMENTUM * new_momentum + mean_delta)
    merged = ALPHA * inner + (1.0 - ALPHA) * new_anchor
    row[1] = merged.astype(BF16).astype(F32)
    line_copies = gather_lines(1)
    results[0] = merged
    results[1] = new_anchor
    results[2] = new_momentum
    stores = [
        pltpu.make_async_copy(results.at[i], out, out_sem.at[i])
        for i, out in enumerate((merged_out, anchor_out, mom_out))
    ]
    for store in stores:
        store.start()
    agy_copies = gather_y(1, line_copies, PARTS)

    for d in range(3):
        agx_copies[d].wait_recv()
        agc_copies.append(
            start(
                copy_to(
                    weights.at[1, x_from[d]], weights.at[0, x_from[d]],
                    agc_ss.at[d + 1], agc_rs.at[d + 1], partner,
                )
            )
        )

    def times_weights(h):
        products = jnp.zeros((256, 128), F32)
        for j in range(CHUNKS):
            for s in range(4):
                products = products + lax.dot_general(
                    cotv[h, j, :, s * 256 : (s + 1) * 256],
                    weights[h, s, :, j * 256 : (j + 1) * 256],
                    (((1,), (1,)), ((), ())), preferred_element_type=F32,
                )
        return products

    products = times_weights(1)

    here = c * 4 + x
    last = []
    for q in range(PARTS):
        for d in range(7):
            agy_copies[7 * q + d].wait_recv()
        ahead_send[q] = jnp.dot(
            ahead, gathered[1, :, q * WIDE : (q + 1) * WIDE], preferred_element_type=F32
        ).astype(BF16)
        for i, (zz, xx, cc) in enumerate(plane):
            last.append(
                start(
                    copy_to(
                        ahead_send.at[q, aligned(xx * 2 + cc, 32)], ahead_out.at[here, q],
                        last_ss.at[q, i], last_rs.at[q, i], at(zz, y, xx, cc),
                    )
                )
            )

    for copy in agc_copies:
        copy.wait_recv()
    products = products + times_weights(0)
    grad_hidden[...] = jnp.dot(
        products.astype(BF16), order, preferred_element_type=F32
    ).astype(BF16)
    store = pltpu.make_async_copy(grad_hidden, grad_hidden_out, out_sem.at[3])
    store.start()
    stores.append(store)

    sources = []
    for dx in range(4):
        for dc in range(2):
            if dx or dc:
                sources.append((lax.rem(x + 4 - dx, 4), 1 - c if dc else c))
    for q in range(PARTS):
        for i in range(-1, 7):
            if i < 0:
                piece = here
                view = ahead_send.at[q, seat]
            else:
                last[7 * q + i].wait_recv()
                piece = sources[i][1] * 4 + sources[i][0]
                view = ahead_out.at[piece, q]
            begin = pl.multiple_of(piece * 1024 + q * WIDE, WIDE)
            store = pltpu.make_async_copy(
                view, next_out.at[:, pl.ds(begin, WIDE)], next_sem.at[q, i + 1]
            )
            store.start()
            stores.append(store)
    for store in stores:
        store.wait()
    for copy in sends:
        copy.wait_send()


def store_kernel(*refs):
    sources, outs, held, sems = refs[:5], refs[5:10], refs[10:15], refs[15]
    inward = [pltpu.make_async_copy(a, b, sems.at[0, i]) for i, (a, b) in enumerate(zip(sources, held))]
    outward = [pltpu.make_async_copy(a, b, sems.at[1, i]) for i, (a, b) in enumerate(zip(held, outs))]
    for copy in inward:
        copy.start()
    for come, go in zip(inward, outward):
        come.wait()
        go.start()
    for copy in outward:
        copy.wait()


def shards(hidden, cotangent, master, adam_m, adam_v, anchor, outer_mom, next_hidden):
    hbm = pl.BlockSpec(memory_space=pltpu.HBM)
    dma = lambda *shape: pltpu.SemaphoreType.DMA(shape)
    row = lambda a: a.reshape(64, 128)
    shapes = (
        jax.ShapeDtypeStruct((256, 128), BF16),
        jax.ShapeDtypeStruct((64, 128), F32),
        jax.ShapeDtypeStruct((64, 128), F32),
        jax.ShapeDtypeStruct((64, 128), F32),
        jax.ShapeDtypeStruct((32, 8192), BF16),
    )
    outs = pl.pallas_call(
        kernel,
        out_shape=shapes,
        in_specs=[hbm] * 8,
        out_specs=(hbm,) * 5,
        scratch_shapes=[
            pltpu.VMEM((256, 128), BF16),
            pltpu.VMEM((3, 64, 128), F32),
            pltpu.VMEM((256, 128), BF16),
            pltpu.VMEM((5, 64, 128), F32),
            pltpu.VMEM((256, 128), BF16),
            pltpu.VMEM((2, CHUNKS, 256, 1024), BF16),
            pltpu.VMEM((CHUNKS, 128, 1024), BF16),
            pltpu.VMEM((CHUNKS, 128, 1024), BF16),
            pltpu.VMEM((CHUNKS, 128, 1024), F32),
            pltpu.VMEM((CHUNKS, 128, 1024), BF16),
            pltpu.VMEM((CHUNKS, 3, 128, 256), BF16),
            pltpu.VMEM((CHUNKS, 128, 256), F32),
            pltpu.VMEM((CHUNKS, 128, 256), BF16),
            pltpu.VMEM((CHUNKS, 7, 16, 256), BF16),
            pltpu.VMEM((128, 128), F32),
            pltpu.VMEM((128, 128), F32),
            pltpu.VMEM((64, 128), F32),
            pltpu.VMEM((4, 64, 128), BF16),
            pltpu.VMEM((2, 64, 128), F32),
            pltpu.VMEM((2, 128, 128), F32),
            pltpu.VMEM((2, 128, 1024), BF16),
            pltpu.VMEM((2, 4, 128, 1024), BF16),
            pltpu.VMEM((PARTS, 256, WIDE), BF16),
            pltpu.VMEM((8, PARTS, 32, WIDE), BF16),
            dma(4), dma(PARTS, 8), dma(3), dma(4), dma(2, CHUNKS, 4), dma(7), dma(7),
            dma(CHUNKS), dma(CHUNKS), dma(CHUNKS, 3), dma(CHUNKS, 3),
            dma(CHUNKS, 7), dma(CHUNKS, 7), dma(15), dma(15), dma(3), dma(3),
            dma(2, 15), dma(2, 15), dma(2, PARTS, 7), dma(2, PARTS, 7),
            dma(3), dma(3), dma(4), dma(4), dma(PARTS, 7), dma(PARTS, 7),
        ],
        compiler_params=pltpu.CompilerParams(
            collective_id=0, has_side_effects=True, vmem_limit_bytes=VMEM_BYTES
        ),
        name="sync",
    )(
        hidden[0], cotangent[0], row(master), row(adam_m), row(adam_v),
        row(anchor), row(outer_mom), next_hidden[0],
    )
    outs = pl.pallas_call(
        store_kernel,
        out_shape=shapes,
        in_specs=[hbm] * 5,
        out_specs=(hbm,) * 5,
        scratch_shapes=[pltpu.VMEM(s.shape, s.dtype) for s in shapes] + [dma(2, 5)],
        compiler_params=pltpu.CompilerParams(vmem_limit_bytes=VMEM_BYTES),
        name="store",
    )(*outs)
    grad_hidden, merged, new_anchor, new_momentum, next_out = outs
    return (
        grad_hidden[None],
        merged.reshape(1, 1, 8192),
        new_anchor.reshape(1, 8192),
        new_momentum.reshape(1, 8192),
        next_out[None],
    )


def solution(mesh):
    in_specs = (
        P("rep", "fsdp", None),
        P("rep", "fsdp", None),
        P("rep", "fsdp", None),
        P("rep", "fsdp", None),
        P("rep", "fsdp", None),
        P("fsdp", None),
        P("fsdp", None),
        P("rep", "fsdp", None),
    )
    out_specs = (
        P("rep", "fsdp", None),
        P("rep", "fsdp", None),
        P("fsdp", None),
        P("fsdp", None),
        P("rep", "fsdp", None),
    )
    return jax.shard_map(shards, mesh=mesh, in_specs=in_specs, out_specs=out_specs, check_vma=False)
```

```python
import math

import jax
import jax.numpy as jnp
from jax import lax
from jax.experimental import pallas as pl
from jax.experimental.pallas import tpu as pltpu
from jax.sharding import PartitionSpec as P

BETA_ONE = 0.9
BETA_TWO = 0.95
INNER_LR = 0.3
DECAY = 0.1
EPS = 1e-08
OUTER_LR = 0.7
MOMENTUM = 0.9
ALPHA = 0.5
STEP = 100

BF16 = jnp.bfloat16
F32 = jnp.float32
VMEM_BYTES = 62 * 1024 * 1024
CHUNKS = 4
PARTS = 2
WIDE = 512 // PARTS
ARRAYS = 24


def row_table():
    p = lax.broadcasted_iota(jnp.int32, (128, 128), 0)
    f = lax.broadcasted_iota(jnp.int32, (128, 128), 1)
    y = lax.shift_right_logical(p, 4)
    z = lax.bitwise_and(lax.shift_right_logical(p, 3), 1)
    return jnp.where(f == z * 64 + y * 8 + lax.bitwise_and(p, 7), 1.0, 0.0).astype(BF16)


def hadamard_table():
    i = lax.broadcasted_iota(jnp.int32, (128, 128), 0)
    j = lax.broadcasted_iota(jnp.int32, (128, 128), 1)
    bits = lax.bitwise_and(i, j)
    bits = lax.bitwise_xor(bits, lax.shift_right_logical(bits, 4))
    bits = lax.bitwise_xor(bits, lax.shift_right_logical(bits, 2))
    bits = lax.bitwise_xor(bits, lax.shift_right_logical(bits, 1))
    return (1 - 2 * lax.bitwise_and(bits, 1)).astype(F32)


def sign_table(first):
    i = lax.broadcasted_iota(jnp.int32, (64, 128), 0)
    j = lax.broadcasted_iota(jnp.int32, (64, 128), 1)
    j = j + 128 * lax.shift_right_logical(i, 4) + first
    return (1 - 2 * lax.rem(lax.rem(97 * j, 251), 2)).astype(F32)


def rotate(values, table):
    out = jnp.dot(
        values, table, precision=lax.Precision.HIGHEST, preferred_element_type=F32
    )
    return out * (1.0 / math.sqrt(128.0))


def copy_to(src, dst, send_sem, recv_sem, device):
    return pltpu.make_async_remote_copy(
        src_ref=src,
        dst_ref=dst,
        send_sem=send_sem,
        recv_sem=recv_sem,
        device_id=device,
        device_id_type=pl.DeviceIdType.MESH,
    )


def aligned(index, size):
    return pl.ds(pl.multiple_of(index * size, size), size)


def kernel(
    hidden_in, cot, master_in, adam_m_in, adam_v_in, anchor_in, outer_mom_in, next_in,
    grad_hidden_out, merged_out, anchor_out, mom_out, next_out,
    grad_hidden, results, hidden, state, next_all, cotv, core_send, core_recv,
    part, x_send, x_recv, x_sum, y_send, y_recv, packed, state_in, rot,
    row16, half_in, half_rows, gathered, back_send, back_recv, weights, ahead_send, ahead_out,
    out_sem, next_sem, in_sem, state_sem, cot_sem, nh_ss, nh_rs, core_ss, core_rs,
    x_ss, x_rs, y_ss, y_rs, st_ss, st_rs, rep_ss, rep_rs, back_ss, back_rs,
    agy_ss, agy_rs, half_ss, half_rs, ring_ss, ring_rs, agc_ss, agc_rs, last_ss, last_rs,
):
    rep = lax.axis_index("rep")
    me = lax.axis_index("fsdp")
    z = lax.div(me, 64)
    y = lax.rem(lax.div(me, 8), 8)
    x = lax.rem(lax.div(me, 2), 4)
    c = lax.rem(me, 2)

    def at(zz, yy, xx, cc):
        return {"fsdp": zz * 64 + yy * 8 + xx * 2 + cc}

    group = []
    for dz in range(2):
        for dx in range(4):
            for dc in range(2):
                if dz or dx or dc:
                    group.append(
                        (1 - z if dz else z, lax.rem(x + dx, 4), 1 - c if dc else c)
                    )
    place = z * 8 + x * 2 + c
    slice_here = c * 8 + x * 2 + z
    partner = at(z, y, x, 1 - c)
    x_peers = [lax.rem(x + d, 4) for d in range(1, 4)]
    x_from = [lax.rem(x + 4 - d, 4) for d in range(1, 4)]
    y_peers = [lax.rem(y + d, 8) for d in range(1, 8)]

    barrier = pltpu.get_barrier_semaphore()
    peers = [at(zz, y, xx, cc) for zz, xx, cc in group]
    peers += [at(z, yy, x, c) for yy in y_peers]
    peers += [at(1 - z, yy, x, c) for yy in y_peers]
    peers += [{"rep": lax.rem(rep + d, 4)} for d in range(1, 4)]
    for peer in peers:
        pl.semaphore_signal(
            barrier, inc=1, device_id=peer, device_id_type=pl.DeviceIdType.MESH
        )

    sends = []

    def start(copy):
        copy.start()
        sends.append(copy)
        return copy

    halves = (1 - c, c)
    seat = aligned(place, 32)
    loads = [
        pltpu.make_async_copy(hidden_in, hidden, in_sem.at[0]),
        pltpu.make_async_copy(master_in, state.at[0], in_sem.at[1]),
        pltpu.make_async_copy(next_in, next_all.at[seat], in_sem.at[2]),
    ]
    for load in loads:
        load.start()
    chunk_at = [(1 - z if j < 2 else z) * 512 + j % 2 * 256 for j in range(CHUNKS)]
    cot_loads = {}
    for h in range(2):
        for j in range(CHUNKS):
            for s in range(4):
                begin = pl.multiple_of(halves[h] * 4096 + s * 1024 + chunk_at[j], 256)
                load = pltpu.make_async_copy(
                    cot.at[:, pl.ds(begin, 256)],
                    cotv.at[h, j, :, pl.ds(s * 256, 256)],
                    cot_sem.at[h, j, s],
                )
                load.start()
                cot_loads[h, j, s] = load
    late_loads = [
        pltpu.make_async_copy(source, state.at[i + 1], state_sem.at[i])
        for i, source in enumerate((adam_m_in, adam_v_in, anchor_in, outer_mom_in))
    ]
    for load in late_loads:
        load.start()

    order = row_table()
    loads[0].wait()
    turned = lax.dot_general(
        order, hidden[...], (((1,), (1,)), ((), ())), preferred_element_type=F32
    ).astype(BF16)

    y_up, y_down = at(z, y_peers[0], x, c), at(z, y_peers[6], x, c)

    def block_of(distance):
        return aligned(lax.rem(y + 8 + distance, 8), 16)

    half_copies, agc_copies, ring = [], [], {}

    def weights_start():
        loads[1].wait()
        row16[...] = state[0].astype(BF16)
        for i, (zz, xx, cc) in enumerate(group):
            half_copies.append(
                start(
                    copy_to(
                        row16.at[aligned(cc, 32)], half_in.at[place],
                        half_ss.at[i], half_rs.at[i], at(zz, y, xx, cc),
                    )
                )
            )
        half_in[place] = row16[aligned(c, 32), :]

    def to_partner(distance):
        i = len(agc_copies)
        block = block_of(distance)
        agc_copies.append(
            start(
                copy_to(
                    weights.at[1, block], weights.at[0, block],
                    agc_ss.at[i], agc_rs.at[i], partner,
                )
            )
        )

    def weights_step(step):
        if step == 1:
            for copy in half_copies:
                copy.wait_recv()
            half_rows[...] = half_in[...].reshape(512, 128).astype(F32)
            for b in range(32):
                block = half_rows[pl.ds(b, 16, stride=32), :]
                weights[1, block_of(0), b * 128 : (b + 1) * 128] = block.astype(BF16)
        for way, device in ((1, y_up), (-1, y_down)):
            side = 0 if way == 1 else 1
            if step > 1:
                ring[step - 1, way].wait_recv()
            if step == 5:
                continue
            view = weights.at[1, block_of(-way * (step - 1))]
            if step == 4:
                view = view.at[:, pl.ds(side * 2048, 2048)]
            ring[step, way] = start(
                copy_to(view, view, ring_ss.at[side, step - 1], ring_rs.at[side, step - 1], device)
            )
        if step == 1:
            to_partner(0)
        elif step == 5:
            to_partner(4)
        else:
            to_partner(1 - step)
            to_partner(step - 1)

    core_copies = []
    for j in range(CHUNKS):
        for s in range(4):
            cot_loads[0, j, s].wait()
        core_send[j] = jnp.dot(turned, cotv[0, j], preferred_element_type=F32).astype(BF16)
        if j == 0:
            pl.semaphore_wait(barrier, len(peers))
        core_copies.append(
            start(
                copy_to(
                    core_send.at[j], core_recv.at[j], core_ss.at[j], core_rs.at[j], partner
                )
            )
        )
    weights_start()

    for load in late_loads:
        load.wait()
    for i in range(16):
        for a in range(5):
            packed[i * ARRAYS + 4 * a : i * ARRAYS + 4 * a + 4, :] = state[a, 4 * i : 4 * i + 4, :]
        packed[i * ARRAYS + 20 : i * ARRAYS + 24, :] = jnp.zeros((4, 128), F32)
    state_copies, nh_copies = [], []
    loads[2].wait()
    for i, (zz, xx, cc) in enumerate(group):
        state_copies.append(
            start(
                copy_to(
                    packed.at[aligned(cc * 8 + xx * 2 + zz, ARRAYS)],
                    state_in.at[aligned(place, ARRAYS)],
                    st_ss.at[i], st_rs.at[i], at(zz, y, xx, cc),
                )
            )
        )
        nh_copies.append(
            start(
                copy_to(
                    next_all.at[seat], next_all.at[seat],
                    nh_ss.at[i], nh_rs.at[i], at(zz, y, xx, cc),
                )
            )
        )
    state_in[aligned(place, ARRAYS), :] = packed[aligned(slice_here, ARRAYS), :]

    x_copies = []
    for j in range(CHUNKS):
        for s in range(4):
            cot_loads[1, j, s].wait()
        own = jnp.dot(turned, cotv[1, j], preferred_element_type=F32)
        core_copies[j].wait_recv()
        both = own + core_recv[j].astype(F32)
        part[j] = both
        x_send[j] = both.astype(BF16)
        for d in range(3):
            x_copies.append(
                start(
                    copy_to(
                        x_send.at[j, :, aligned(x_peers[d], 256)], x_recv.at[j, d],
                        x_ss.at[j, d], x_rs.at[j, d], at(z, y, x_peers[d], c),
                    )
                )
            )

    weights_step(1)

    rs_y = {}
    for j in range(CHUNKS):
        total = part[j, :, aligned(x, 256)]
        for d in range(3):
            x_copies[3 * j + d].wait_recv()
            total = total + x_recv[j, d].astype(F32)
        x_sum[j] = total
        y_send[j] = total.astype(BF16)
        for d in range(8):
            if d == 0 and j >= 2:
                continue
            yy = lax.rem(y + d, 8)
            rs_y[j, d] = start(
                copy_to(
                    y_send.at[j, aligned(yy, 16)], y_recv.at[j, d],
                    y_ss.at[j, d], y_rs.at[j, d], at(1 - z if j < 2 else z, yy, x, c),
                )
            )
        weights_step(j + 2)

    table = hadamard_table()
    signs = sign_table(c * 4096 + x * 1024 + z * 512)
    for copy in state_copies:
        copy.wait_recv()
    master, adam_m, adam_v, anchor, outer_mom = (
        jnp.concatenate(
            [state_in[pl.ds(4 * a + b, 16, stride=ARRAYS), :] for b in range(4)], axis=0
        )
        for a in range(5)
    )
    sums = []
    for k in range(2):
        total = x_sum[2 + k, aligned(y, 16), :]
        for j in (k, 2 + k):
            for d in range(8):
                if (j, d) in rs_y:
                    rs_y[j, d].wait_recv()
                    total = total + y_recv[j, d].astype(F32)
        sums += [total[:, :128], total[:, 128:]]
    gradient = jnp.concatenate(sums, axis=0)

    first = BETA_ONE * adam_m + (1.0 - BETA_ONE) * gradient
    second = BETA_TWO * adam_v + (1.0 - BETA_TWO) * gradient * gradient
    corr_one = 1.0 - BETA_ONE**STEP
    corr_two = 1.0 - BETA_TWO**STEP
    update = first / corr_one / (jnp.sqrt(second / corr_two) + EPS) + DECAY * master
    inner = master - INNER_LR * update
    rot[rep] = rotate((anchor - inner) * signs, table).astype(BF16)
    rep_copies = []
    for d in range(3):
        rep_copies.append(
            start(
                copy_to(
                    rot.at[rep], rot.at[rep], rep_ss.at[d], rep_rs.at[d],
                    {"rep": lax.rem(rep + d + 1, 4)},
                )
            )
        )
    for copy in nh_copies:
        copy.wait_recv()
    ahead = lax.dot_general(
        next_all[...], order, (((1,), (1,)), ((), ())), preferred_element_type=F32
    ).astype(BF16)
    for copy in rep_copies:
        copy.wait_recv()
    total = rot[0].astype(F32)
    for r in range(1, 4):
        total = total + rot[r].astype(F32)
    mean_delta = rotate(total, table) * signs * 0.25
    new_momentum = MOMENTUM * outer_mom + mean_delta
    new_anchor = anchor - OUTER_LR * (MOMENTUM * new_momentum + mean_delta)
    merged = ALPHA * inner + (1.0 - ALPHA) * new_anchor
    rows = aligned(y, 16)
    for b in range(4):
        gathered[rows, b * 128 : (b + 1) * 128] = merged[16 * b : 16 * b + 16].astype(BF16)
    agy_copies, stores = [], []
    for q in range(PARTS):
        view = gathered.at[rows, pl.ds(q * WIDE, WIDE)]
        for d in range(7):
            agy_copies.append(
                start(
                    copy_to(
                        view, view, agy_ss.at[q, d], agy_rs.at[q, d], at(z, y_peers[d], x, c)
                    )
                )
            )

    for a, value in enumerate((merged, new_anchor, new_momentum, jnp.zeros((64, 128), F32))):
        for b in range(4):
            back_send[pl.ds(4 * a + b, 16, stride=16), :] = value[16 * b : 16 * b + 16]
    back_copies = []
    for i, (zz, xx, cc) in enumerate(group):
        back_copies.append(
            start(
                copy_to(
                    back_send.at[aligned(zz * 8 + xx * 2 + cc, 16)],
                    back_recv.at[aligned(slice_here, 16)],
                    back_ss.at[i], back_rs.at[i], at(zz, y, xx, cc),
                )
            )
        )
    back_recv[aligned(slice_here, 16), :] = back_send[aligned(place, 16), :]

    def times_weights(h):
        products = jnp.zeros((256, 128), F32)
        for j in range(CHUNKS):
            for s in range(4):
                products = products + lax.dot_general(
                    cotv[h, j, :, s * 256 : (s + 1) * 256],
                    weights[h, :, aligned(s * 4 + lax.div(chunk_at[j], 256), 256)],
                    (((1,), (1,)), ((), ())), preferred_element_type=F32,
                )
        return products

    products = times_weights(1)

    last = []
    for q in range(PARTS):
        for d in range(7):
            agy_copies[7 * q + d].wait_recv()
        ahead_send[q] = jnp.dot(
            ahead, gathered[:, q * WIDE : (q + 1) * WIDE], preferred_element_type=F32
        ).astype(BF16)
        for i, (zz, xx, cc) in enumerate(group):
            last.append(
                start(
                    copy_to(
                        ahead_send.at[q, aligned(zz * 8 + xx * 2 + cc, 32)],
                        ahead_out.at[slice_here, q],
                        last_ss.at[q, i], last_rs.at[q, i], at(zz, y, xx, cc),
                    )
                )
            )

    for copy in agc_copies:
        copy.wait_recv()
    products = products + times_weights(0)
    grad_hidden[...] = jnp.dot(
        products.astype(BF16), order, preferred_element_type=F32
    ).astype(BF16)
    store = pltpu.make_async_copy(grad_hidden, grad_hidden_out, out_sem.at[3])
    store.start()
    stores.append(store)

    for copy in back_copies:
        copy.wait_recv()
    for a, out in enumerate((merged_out, anchor_out, mom_out)):
        for i in range(16):
            results[a, 4 * i : 4 * i + 4, :] = back_recv[16 * i + 4 * a : 16 * i + 4 * a + 4, :]
        store = pltpu.make_async_copy(results.at[a], out, out_sem.at[a])
        store.start()
        stores.append(store)

    sources = [slice_here]
    for dz in range(2):
        for dx in range(4):
            for dc in range(2):
                if dz or dx or dc:
                    sources.append(
                        (1 - c if dc else c) * 8
                        + lax.rem(x + 4 - dx, 4) * 2
                        + (1 - z if dz else z)
                    )
    for q in range(PARTS):
        for i, piece in enumerate(sources):
            view = ahead_send.at[q, seat]
            if i:
                last[15 * q + i - 1].wait_recv()
                view = ahead_out.at[piece, q]
            begin = pl.multiple_of(piece * 512 + q * WIDE, WIDE)
            store = pltpu.make_async_copy(
                view, next_out.at[:, pl.ds(begin, WIDE)], next_sem.at[q, i]
            )
            store.start()
            stores.append(store)
    for store in stores:
        store.wait()
    for copy in sends:
        copy.wait_send()


def store_kernel(*refs):
    sources, outs, held, sems = refs[:5], refs[5:10], refs[10:15], refs[15]
    inward = [pltpu.make_async_copy(a, b, sems.at[0, i]) for i, (a, b) in enumerate(zip(sources, held))]
    outward = [pltpu.make_async_copy(a, b, sems.at[1, i]) for i, (a, b) in enumerate(zip(held, outs))]
    for copy in inward:
        copy.start()
    for come, go in zip(inward, outward):
        come.wait()
        go.start()
    for copy in outward:
        copy.wait()


def shards(hidden, cotangent, master, adam_m, adam_v, anchor, outer_mom, next_hidden):
    hbm = pl.BlockSpec(memory_space=pltpu.HBM)
    dma = lambda *shape: pltpu.SemaphoreType.DMA(shape)
    row = lambda a: a.reshape(64, 128)
    shapes = (
        jax.ShapeDtypeStruct((256, 128), BF16),
        jax.ShapeDtypeStruct((64, 128), F32),
        jax.ShapeDtypeStruct((64, 128), F32),
        jax.ShapeDtypeStruct((64, 128), F32),
        jax.ShapeDtypeStruct((32, 8192), BF16),
    )
    outs = pl.pallas_call(
        kernel,
        out_shape=shapes,
        in_specs=[hbm] * 8,
        out_specs=(hbm,) * 5,
        scratch_shapes=[
            pltpu.VMEM((256, 128), BF16),
            pltpu.VMEM((3, 64, 128), F32),
            pltpu.VMEM((256, 128), BF16),
            pltpu.VMEM((5, 64, 128), F32),
            pltpu.VMEM((512, 128), BF16),
            pltpu.VMEM((2, CHUNKS, 256, 1024), BF16),
            pltpu.VMEM((CHUNKS, 128, 1024), BF16),
            pltpu.VMEM((CHUNKS, 128, 1024), BF16),
            pltpu.VMEM((CHUNKS, 128, 1024), F32),
            pltpu.VMEM((CHUNKS, 128, 1024), BF16),
            pltpu.VMEM((CHUNKS, 3, 128, 256), BF16),
            pltpu.VMEM((CHUNKS, 128, 256), F32),
            pltpu.VMEM((CHUNKS, 128, 256), BF16),
            pltpu.VMEM((CHUNKS, 8, 16, 256), BF16),
            pltpu.VMEM((16 * ARRAYS, 128), F32),
            pltpu.VMEM((16 * ARRAYS, 128), F32),
            pltpu.VMEM((4, 64, 128), BF16),
            pltpu.VMEM((64, 128), BF16),
            pltpu.VMEM((16, 32, 128), BF16),
            pltpu.VMEM((512, 128), F32),
            pltpu.VMEM((128, 512), BF16),
            pltpu.VMEM((256, 128), F32),
            pltpu.VMEM((256, 128), F32),
            pltpu.VMEM((2, 128, 4096), BF16),
            pltpu.VMEM((PARTS, 512, WIDE), BF16),
            pltpu.VMEM((16, PARTS, 32, WIDE), BF16),
            dma(4), dma(PARTS, 16), dma(3), dma(4), dma(2, CHUNKS, 4), dma(15), dma(15),
            dma(CHUNKS), dma(CHUNKS), dma(CHUNKS, 3), dma(CHUNKS, 3),
            dma(CHUNKS, 8), dma(CHUNKS, 8), dma(15), dma(15), dma(3), dma(3),
            dma(15), dma(15), dma(PARTS, 7), dma(PARTS, 7), dma(15), dma(15),
            dma(2, 4), dma(2, 4), dma(8), dma(8), dma(PARTS, 15), dma(PARTS, 15),
        ],
        compiler_params=pltpu.CompilerParams(
            collective_id=0, has_side_effects=True, vmem_limit_bytes=VMEM_BYTES
        ),
        name="sync",
    )(
        hidden[0], cotangent[0], row(master), row(adam_m), row(adam_v),
        row(anchor), row(outer_mom), next_hidden[0],
    )
    outs = pl.pallas_call(
        store_kernel,
        out_shape=shapes,
        in_specs=[hbm] * 5,
        out_specs=(hbm,) * 5,
        scratch_shapes=[pltpu.VMEM(s.shape, s.dtype) for s in shapes] + [dma(2, 5)],
        compiler_params=pltpu.CompilerParams(vmem_limit_bytes=VMEM_BYTES),
        name="store",
    )(*outs)
    grad_hidden, merged, new_anchor, new_momentum, next_out = outs
    return (
        grad_hidden[None],
        merged.reshape(1, 1, 8192),
        new_anchor.reshape(1, 8192),
        new_momentum.reshape(1, 8192),
        next_out[None],
    )


def solution(mesh):
    in_specs = (
        P("rep", "fsdp", None),
        P("rep", "fsdp", None),
        P("rep", "fsdp", None),
        P("rep", "fsdp", None),
        P("rep", "fsdp", None),
        P("fsdp", None),
        P("fsdp", None),
        P("rep", "fsdp", None),
    )
    out_specs = (
        P("rep", "fsdp", None),
        P("rep", "fsdp", None),
        P("fsdp", None),
        P("fsdp", None),
        P("rep", "fsdp", None),
    )
    return jax.shard_map(shards, mesh=mesh, in_specs=in_specs, out_specs=out_specs, check_vma=False)
```

```python
import math

import jax
import jax.numpy as jnp
from jax import lax
from jax.experimental import pallas as pl
from jax.experimental.pallas import tpu as pltpu
from jax.sharding import PartitionSpec as P

BETA_ONE = 0.9
BETA_TWO = 0.95
INNER_LR = 0.3
DECAY = 0.1
EPS = 1e-08
OUTER_LR = 0.7
MOMENTUM = 0.9
ALPHA = 0.5
STEP = 100

BF16 = jnp.bfloat16
F32 = jnp.float32
VMEM_BYTES = 62 * 1024 * 1024
CHUNKS = 4
PARTS = 2
WIDE = 512 // PARTS
ARRAYS = 24


def row_table():
    p = lax.broadcasted_iota(jnp.int32, (128, 128), 0)
    f = lax.broadcasted_iota(jnp.int32, (128, 128), 1)
    y = lax.shift_right_logical(p, 4)
    z = lax.bitwise_and(lax.shift_right_logical(p, 3), 1)
    return jnp.where(f == z * 64 + y * 8 + lax.bitwise_and(p, 7), 1.0, 0.0).astype(BF16)


def hadamard_table():
    i = lax.broadcasted_iota(jnp.int32, (128, 128), 0)
    j = lax.broadcasted_iota(jnp.int32, (128, 128), 1)
    bits = lax.bitwise_and(i, j)
    bits = lax.bitwise_xor(bits, lax.shift_right_logical(bits, 4))
    bits = lax.bitwise_xor(bits, lax.shift_right_logical(bits, 2))
    bits = lax.bitwise_xor(bits, lax.shift_right_logical(bits, 1))
    return (1 - 2 * lax.bitwise_and(bits, 1)).astype(F32)


def sign_table(first):
    i = lax.broadcasted_iota(jnp.int32, (64, 128), 0)
    j = lax.broadcasted_iota(jnp.int32, (64, 128), 1)
    j = j + 128 * lax.shift_right_logical(i, 4) + first
    return (1 - 2 * lax.rem(lax.rem(97 * j, 251), 2)).astype(F32)


def rotate(values, table):
    out = jnp.dot(
        values, table, precision=lax.Precision.HIGHEST, preferred_element_type=F32
    )
    return out * (1.0 / math.sqrt(128.0))


def copy_to(src, dst, send_sem, recv_sem, device):
    return pltpu.make_async_remote_copy(
        src_ref=src,
        dst_ref=dst,
        send_sem=send_sem,
        recv_sem=recv_sem,
        device_id=device,
        device_id_type=pl.DeviceIdType.MESH,
    )


def aligned(index, size):
    return pl.ds(pl.multiple_of(index * size, size), size)


def kernel(
    hidden_in, cot, master_in, adam_m_in, adam_v_in, anchor_in, outer_mom_in, next_in,
    grad_hidden_out, merged_out, anchor_out, mom_out, next_out,
    grad_hidden, results, hidden, state, next_all, cotv, core_send, core_recv,
    part, x_send, x_recv, x_sum, y_send, y_recv, packed, state_in, rot,
    row16, half_in, half_rows, gathered, back_send, back_recv, weights, ahead_send, ahead_out,
    out_sem, next_sem, in_sem, state_sem, cot_sem, nh_ss, nh_rs, core_ss, core_rs,
    x_ss, x_rs, y_ss, y_rs, st_ss, st_rs, rep_ss, rep_rs, back_ss, back_rs,
    agy_ss, agy_rs, half_ss, half_rs, ring_ss, ring_rs, agc_ss, agc_rs, last_ss, last_rs,
):
    rep = lax.axis_index("rep")
    me = lax.axis_index("fsdp")
    z = lax.div(me, 64)
    y = lax.rem(lax.div(me, 8), 8)
    x = lax.rem(lax.div(me, 2), 4)
    c = lax.rem(me, 2)

    def at(zz, yy, xx, cc):
        return {"fsdp": zz * 64 + yy * 8 + xx * 2 + cc}

    group = []
    for dz in range(2):
        for dx in range(4):
            for dc in range(2):
                if dz or dx or dc:
                    group.append(
                        (1 - z if dz else z, lax.rem(x + dx, 4), 1 - c if dc else c)
                    )
    place = z * 8 + x * 2 + c
    slice_here = c * 8 + x * 2 + z
    partner = at(z, y, x, 1 - c)
    x_peers = [lax.rem(x + d, 4) for d in range(1, 4)]
    x_from = [lax.rem(x + 4 - d, 4) for d in range(1, 4)]
    y_peers = [lax.rem(y + d, 8) for d in range(1, 8)]

    barrier = pltpu.get_barrier_semaphore()
    peers = [at(zz, y, xx, cc) for zz, xx, cc in group]
    peers += [at(z, yy, x, c) for yy in y_peers]
    peers += [at(1 - z, yy, x, c) for yy in y_peers]
    peers += [{"rep": lax.rem(rep + d, 4)} for d in range(1, 4)]
    for peer in peers:
        pl.semaphore_signal(
            barrier, inc=1, device_id=peer, device_id_type=pl.DeviceIdType.MESH
        )

    sends = []

    def start(copy):
        copy.start()
        sends.append(copy)
        return copy

    halves = (1 - c, c)
    seat = aligned(place, 32)
    loads = [
        pltpu.make_async_copy(hidden_in, hidden, in_sem.at[0]),
        pltpu.make_async_copy(master_in, state.at[0], in_sem.at[1]),
        pltpu.make_async_copy(next_in, next_all.at[seat], in_sem.at[2]),
    ]
    for load in loads:
        load.start()
    chunk_at = [(1 - z if j < 2 else z) * 512 + j % 2 * 256 for j in range(CHUNKS)]
    cot_loads = {}
    for j in range(CHUNKS):
        for h in range(2):
            for s in range(4):
                begin = pl.multiple_of(halves[h] * 4096 + s * 1024 + chunk_at[j], 256)
                load = pltpu.make_async_copy(
                    cot.at[:, pl.ds(begin, 256)],
                    cotv.at[h, j, :, pl.ds(s * 256, 256)],
                    cot_sem.at[h, j, s],
                )
                load.start()
                cot_loads[h, j, s] = load
    late_loads = [
        pltpu.make_async_copy(source, state.at[i + 1], state_sem.at[i])
        for i, source in enumerate((adam_m_in, adam_v_in, anchor_in, outer_mom_in))
    ]
    for load in late_loads:
        load.start()

    order = row_table()
    loads[0].wait()
    turned = lax.dot_general(
        order, hidden[...], (((1,), (1,)), ((), ())), preferred_element_type=F32
    ).astype(BF16)

    y_up, y_down = at(z, y_peers[0], x, c), at(z, y_peers[6], x, c)

    def block_of(distance):
        return aligned(lax.rem(y + 8 + distance, 8), 16)

    half_copies, agc_copies, ring = [], [], {}

    def weights_start():
        loads[1].wait()
        row16[...] = state[0].astype(BF16)
        for i, (zz, xx, cc) in enumerate(group):
            half_copies.append(
                start(
                    copy_to(
                        row16.at[aligned(cc, 32)], half_in.at[place],
                        half_ss.at[i], half_rs.at[i], at(zz, y, xx, cc),
                    )
                )
            )
        half_in[place] = row16[aligned(c, 32), :]

    def to_partner(distance):
        i = len(agc_copies)
        block = block_of(distance)
        agc_copies.append(
            start(
                copy_to(
                    weights.at[1, block], weights.at[0, block],
                    agc_ss.at[i], agc_rs.at[i], partner,
                )
            )
        )

    def weights_step(step):
        if step == 1:
            for copy in half_copies:
                copy.wait_recv()
            half_rows[...] = half_in[...].reshape(512, 128).astype(F32)
            for b in range(32):
                block = half_rows[pl.ds(b, 16, stride=32), :]
                weights[1, block_of(0), b * 128 : (b + 1) * 128] = block.astype(BF16)
        for way, device in ((1, y_up), (-1, y_down)):
            side = 0 if way == 1 else 1
            if step > 1:
                ring[step - 1, way].wait_recv()
            if step == 5:
                continue
            view = weights.at[1, block_of(-way * (step - 1))]
            if step == 4:
                view = view.at[:, pl.ds(side * 2048, 2048)]
            ring[step, way] = start(
                copy_to(view, view, ring_ss.at[side, step - 1], ring_rs.at[side, step - 1], device)
            )
        if step == 1:
            to_partner(0)
        elif step == 5:
            to_partner(4)
        else:
            to_partner(1 - step)
            to_partner(step - 1)

    core_copies = []
    x_copies = []

    def chunk_to_x(j):
        for s in range(4):
            cot_loads[1, j, s].wait()
        own = jnp.dot(turned, cotv[1, j], preferred_element_type=F32)
        core_copies[j].wait_recv()
        both = own + core_recv[j].astype(F32)
        part[j] = both
        x_send[j] = both.astype(BF16)
        for d in range(3):
            x_copies.append(
                start(
                    copy_to(
                        x_send.at[j, :, aligned(x_peers[d], 256)], x_recv.at[j, d],
                        x_ss.at[j, d], x_rs.at[j, d], at(z, y, x_peers[d], c),
                    )
                )
            )

    for j in range(CHUNKS):
        for s in range(4):
            cot_loads[0, j, s].wait()
        core_send[j] = jnp.dot(turned, cotv[0, j], preferred_element_type=F32).astype(BF16)
        if j == 0:
            pl.semaphore_wait(barrier, len(peers))
            weights_start()
        core_copies.append(
            start(
                copy_to(
                    core_send.at[j], core_recv.at[j], core_ss.at[j], core_rs.at[j], partner
                )
            )
        )
        if j:
            chunk_to_x(j - 1)
    chunk_to_x(CHUNKS - 1)
    weights_step(1)

    for load in late_loads:
        load.wait()
    for i in range(16):
        for a in range(5):
            packed[i * ARRAYS + 4 * a : i * ARRAYS + 4 * a + 4, :] = state[a, 4 * i : 4 * i + 4, :]
        packed[i * ARRAYS + 20 : i * ARRAYS + 24, :] = jnp.zeros((4, 128), F32)
    state_copies = []
    for i, (zz, xx, cc) in enumerate(group):
        state_copies.append(
            start(
                copy_to(
                    packed.at[aligned(cc * 8 + xx * 2 + zz, ARRAYS)],
                    state_in.at[aligned(place, ARRAYS)],
                    st_ss.at[i], st_rs.at[i], at(zz, y, xx, cc),
                )
            )
        )
    state_in[aligned(place, ARRAYS), :] = packed[aligned(slice_here, ARRAYS), :]

    rs_y = {}
    for j in range(CHUNKS):
        total = part[j, :, aligned(x, 256)]
        for d in range(3):
            x_copies[3 * j + d].wait_recv()
            total = total + x_recv[j, d].astype(F32)
        x_sum[j] = total
        y_send[j] = total.astype(BF16)
        for d in range(8):
            if d == 0 and j >= 2:
                continue
            yy = lax.rem(y + d, 8)
            rs_y[j, d] = start(
                copy_to(
                    y_send.at[j, aligned(yy, 16)], y_recv.at[j, d],
                    y_ss.at[j, d], y_rs.at[j, d], at(1 - z if j < 2 else z, yy, x, c),
                )
            )
        if j == 0:
            weights_step(2)

    table = hadamard_table()
    signs = sign_table(c * 4096 + x * 1024 + z * 512)
    for copy in state_copies:
        copy.wait_recv()
    master, adam_m, adam_v, anchor, outer_mom = (
        jnp.concatenate(
            [state_in[pl.ds(4 * a + b, 16, stride=ARRAYS), :] for b in range(4)], axis=0
        )
        for a in range(5)
    )
    sums = []
    for k in range(2):
        total = x_sum[2 + k, aligned(y, 16), :]
        for j in (k, 2 + k):
            for d in range(8):
                if (j, d) in rs_y:
                    rs_y[j, d].wait_recv()
                    total = total + y_recv[j, d].astype(F32)
        sums += [total[:, :128], total[:, 128:]]
    gradient = jnp.concatenate(sums, axis=0)

    first = BETA_ONE * adam_m + (1.0 - BETA_ONE) * gradient
    second = BETA_TWO * adam_v + (1.0 - BETA_TWO) * gradient * gradient
    corr_one = 1.0 - BETA_ONE**STEP
    corr_two = 1.0 - BETA_TWO**STEP
    update = first / corr_one / (jnp.sqrt(second / corr_two) + EPS) + DECAY * master
    inner = master - INNER_LR * update
    rot[rep] = rotate((anchor - inner) * signs, table).astype(BF16)
    rep_copies = []
    for d in range(3):
        rep_copies.append(
            start(
                copy_to(
                    rot.at[rep], rot.at[rep], rep_ss.at[d], rep_rs.at[d],
                    {"rep": lax.rem(rep + d + 1, 4)},
                )
            )
        )
    weights_step(3)
    loads[2].wait()
    nh_copies = []
    for i, (zz, xx, cc) in enumerate(group):
        nh_copies.append(
            start(
                copy_to(
                    next_all.at[seat], next_all.at[seat],
                    nh_ss.at[i], nh_rs.at[i], at(zz, y, xx, cc),
                )
            )
        )
    for copy in rep_copies:
        copy.wait_recv()
    total = rot[0].astype(F32)
    for r in range(1, 4):
        total = total + rot[r].astype(F32)
    mean_delta = rotate(total, table) * signs * 0.25
    new_momentum = MOMENTUM * outer_mom + mean_delta
    new_anchor = anchor - OUTER_LR * (MOMENTUM * new_momentum + mean_delta)
    merged = ALPHA * inner + (1.0 - ALPHA) * new_anchor
    rows = aligned(y, 16)
    for b in range(4):
        gathered[rows, b * 128 : (b + 1) * 128] = merged[16 * b : 16 * b + 16].astype(BF16)
    agy_copies, stores = [], []
    for q in range(PARTS):
        view = gathered.at[rows, pl.ds(q * WIDE, WIDE)]
        for d in range(7):
            agy_copies.append(
                start(
                    copy_to(
                        view, view, agy_ss.at[q, d], agy_rs.at[q, d], at(z, y_peers[d], x, c)
                    )
                )
            )

    for a, value in enumerate((merged, new_anchor, new_momentum, jnp.zeros((64, 128), F32))):
        for b in range(4):
            back_send[pl.ds(4 * a + b, 16, stride=16), :] = value[16 * b : 16 * b + 16]
    back_copies = []
    for i, (zz, xx, cc) in enumerate(group):
        back_copies.append(
            start(
                copy_to(
                    back_send.at[aligned(zz * 8 + xx * 2 + cc, 16)],
                    back_recv.at[aligned(slice_here, 16)],
                    back_ss.at[i], back_rs.at[i], at(zz, y, xx, cc),
                )
            )
        )
    back_recv[aligned(slice_here, 16), :] = back_send[aligned(place, 16), :]

    def times_weights(h):
        products = jnp.zeros((256, 128), F32)
        for j in range(CHUNKS):
            for s in range(4):
                products = products + lax.dot_general(
                    cotv[h, j, :, s * 256 : (s + 1) * 256],
                    weights[h, :, aligned(s * 4 + lax.div(chunk_at[j], 256), 256)],
                    (((1,), (1,)), ((), ())), preferred_element_type=F32,
                )
        return products

    for copy in nh_copies:
        copy.wait_recv()
    ahead = lax.dot_general(
        next_all[...], order, (((1,), (1,)), ((), ())), preferred_element_type=F32
    ).astype(BF16)
    weights_step(4)

    last = []
    for q in range(PARTS):
        for d in range(7):
            agy_copies[7 * q + d].wait_recv()
        ahead_send[q] = jnp.dot(
            ahead, gathered[:, q * WIDE : (q + 1) * WIDE], preferred_element_type=F32
        ).astype(BF16)
        for i, (zz, xx, cc) in enumerate(group):
            last.append(
                start(
                    copy_to(
                        ahead_send.at[q, aligned(zz * 8 + xx * 2 + cc, 32)],
                        ahead_out.at[slice_here, q],
                        last_ss.at[q, i], last_rs.at[q, i], at(zz, y, xx, cc),
                    )
                )
            )

    weights_step(5)
    products = times_weights(1)
    for copy in agc_copies:
        copy.wait_recv()
    products = products + times_weights(0)
    grad_hidden[...] = jnp.dot(
        products.astype(BF16), order, preferred_element_type=F32
    ).astype(BF16)
    store = pltpu.make_async_copy(grad_hidden, grad_hidden_out, out_sem.at[3])
    store.start()
    stores.append(store)

    for copy in back_copies:
        copy.wait_recv()
    for a, out in enumerate((merged_out, anchor_out, mom_out)):
        for i in range(16):
            results[a, 4 * i : 4 * i + 4, :] = back_recv[16 * i + 4 * a : 16 * i + 4 * a + 4, :]
        store = pltpu.make_async_copy(results.at[a], out, out_sem.at[a])
        store.start()
        stores.append(store)

    sources = [slice_here]
    for dz in range(2):
        for dx in range(4):
            for dc in range(2):
                if dz or dx or dc:
                    sources.append(
                        (1 - c if dc else c) * 8
                        + lax.rem(x + 4 - dx, 4) * 2
                        + (1 - z if dz else z)
                    )
    for q in range(PARTS):
        for i, piece in enumerate(sources):
            view = ahead_send.at[q, seat]
            if i:
                last[15 * q + i - 1].wait_recv()
                view = ahead_out.at[piece, q]
            begin = pl.multiple_of(piece * 512 + q * WIDE, WIDE)
            store = pltpu.make_async_copy(
                view, next_out.at[:, pl.ds(begin, WIDE)], next_sem.at[q, i]
            )
            store.start()
            stores.append(store)
    for store in stores:
        store.wait()
    for copy in sends:
        copy.wait_send()


def store_kernel(*refs):
    sources, outs, held, sems = refs[:5], refs[5:10], refs[10:15], refs[15]
    inward = [pltpu.make_async_copy(a, b, sems.at[0, i]) for i, (a, b) in enumerate(zip(sources, held))]
    outward = [pltpu.make_async_copy(a, b, sems.at[1, i]) for i, (a, b) in enumerate(zip(held, outs))]
    for copy in inward:
        copy.start()
    for come, go in zip(inward, outward):
        come.wait()
        go.start()
    for copy in outward:
        copy.wait()


def shards(hidden, cotangent, master, adam_m, adam_v, anchor, outer_mom, next_hidden):
    hbm = pl.BlockSpec(memory_space=pltpu.HBM)
    dma = lambda *shape: pltpu.SemaphoreType.DMA(shape)
    row = lambda a: a.reshape(64, 128)
    shapes = (
        jax.ShapeDtypeStruct((256, 128), BF16),
        jax.ShapeDtypeStruct((64, 128), F32),
        jax.ShapeDtypeStruct((64, 128), F32),
        jax.ShapeDtypeStruct((64, 128), F32),
        jax.ShapeDtypeStruct((32, 8192), BF16),
    )
    outs = pl.pallas_call(
        kernel,
        out_shape=shapes,
        in_specs=[hbm] * 8,
        out_specs=(hbm,) * 5,
        scratch_shapes=[
            pltpu.VMEM((256, 128), BF16),
            pltpu.VMEM((3, 64, 128), F32),
            pltpu.VMEM((256, 128), BF16),
            pltpu.VMEM((5, 64, 128), F32),
            pltpu.VMEM((512, 128), BF16),
            pltpu.VMEM((2, CHUNKS, 256, 1024), BF16),
            pltpu.VMEM((CHUNKS, 128, 1024), BF16),
            pltpu.VMEM((CHUNKS, 128, 1024), BF16),
            pltpu.VMEM((CHUNKS, 128, 1024), F32),
            pltpu.VMEM((CHUNKS, 128, 1024), BF16),
            pltpu.VMEM((CHUNKS, 3, 128, 256), BF16),
            pltpu.VMEM((CHUNKS, 128, 256), F32),
            pltpu.VMEM((CHUNKS, 128, 256), BF16),
            pltpu.VMEM((CHUNKS, 8, 16, 256), BF16),
            pltpu.VMEM((16 * ARRAYS, 128), F32),
            pltpu.VMEM((16 * ARRAYS, 128), F32),
            pltpu.VMEM((4, 64, 128), BF16),
            pltpu.VMEM((64, 128), BF16),
            pltpu.VMEM((16, 32, 128), BF16),
            pltpu.VMEM((512, 128), F32),
            pltpu.VMEM((128, 512), BF16),
            pltpu.VMEM((256, 128), F32),
            pltpu.VMEM((256, 128), F32),
            pltpu.VMEM((2, 128, 4096), BF16),
            pltpu.VMEM((PARTS, 512, WIDE), BF16),
            pltpu.VMEM((16, PARTS, 32, WIDE), BF16),
            dma(4), dma(PARTS, 16), dma(3), dma(4), dma(2, CHUNKS, 4), dma(15), dma(15),
            dma(CHUNKS), dma(CHUNKS), dma(CHUNKS, 3), dma(CHUNKS, 3),
            dma(CHUNKS, 8), dma(CHUNKS, 8), dma(15), dma(15), dma(3), dma(3),
            dma(15), dma(15), dma(PARTS, 7), dma(PARTS, 7), dma(15), dma(15),
            dma(2, 4), dma(2, 4), dma(8), dma(8), dma(PARTS, 15), dma(PARTS, 15),
        ],
        compiler_params=pltpu.CompilerParams(
            collective_id=0, has_side_effects=True, vmem_limit_bytes=VMEM_BYTES
        ),
        name="sync",
    )(
        hidden[0], cotangent[0], row(master), row(adam_m), row(adam_v),
        row(anchor), row(outer_mom), next_hidden[0],
    )
    outs = pl.pallas_call(
        store_kernel,
        out_shape=shapes,
        in_specs=[hbm] * 5,
        out_specs=(hbm,) * 5,
        scratch_shapes=[pltpu.VMEM(s.shape, s.dtype) for s in shapes] + [dma(2, 5)],
        compiler_params=pltpu.CompilerParams(vmem_limit_bytes=VMEM_BYTES),
        name="store",
    )(*outs)
    grad_hidden, merged, new_anchor, new_momentum, next_out = outs
    return (
        grad_hidden[None],
        merged.reshape(1, 1, 8192),
        new_anchor.reshape(1, 8192),
        new_momentum.reshape(1, 8192),
        next_out[None],
    )


def solution(mesh):
    in_specs = (
        P("rep", "fsdp", None),
        P("rep", "fsdp", None),
        P("rep", "fsdp", None),
        P("rep", "fsdp", None),
        P("rep", "fsdp", None),
        P("fsdp", None),
        P("fsdp", None),
        P("rep", "fsdp", None),
    )
    out_specs = (
        P("rep", "fsdp", None),
        P("rep", "fsdp", None),
        P("fsdp", None),
        P("fsdp", None),
        P("rep", "fsdp", None),
    )
    return jax.shard_map(shards, mesh=mesh, in_specs=in_specs, out_specs=out_specs, check_vma=False)
```

```python
import math

import jax
import jax.numpy as jnp
from jax import lax
from jax.experimental import pallas as pl
from jax.experimental.pallas import tpu as pltpu
from jax.sharding import PartitionSpec as P

BETA_ONE = 0.9
BETA_TWO = 0.95
INNER_LR = 0.3
DECAY = 0.1
EPS = 1e-08
OUTER_LR = 0.7
MOMENTUM = 0.9
ALPHA = 0.5
STEP = 100

BF16 = jnp.bfloat16
F32 = jnp.float32
VMEM_BYTES = 62 * 1024 * 1024
CHUNKS = 4
PARTS = 2
WIDE = 512 // PARTS
OFFSETS = sorted(
    ((dz, dx, dc) for dz in range(2) for dx in range(4) for dc in range(2) if dz or dx or dc),
    key=lambda offset: -(offset[0] + min(offset[1], 4 - offset[1])),
)
FAR_Y = (4, 3, 5, 2, 6, 1, 7)
FAR_X = (1, 0, 2)
ARRAYS = 24


def row_table():
    p = lax.broadcasted_iota(jnp.int32, (128, 128), 0)
    f = lax.broadcasted_iota(jnp.int32, (128, 128), 1)
    y = lax.shift_right_logical(p, 4)
    z = lax.bitwise_and(lax.shift_right_logical(p, 3), 1)
    return jnp.where(f == z * 64 + y * 8 + lax.bitwise_and(p, 7), 1.0, 0.0).astype(BF16)


def hadamard_table():
    i = lax.broadcasted_iota(jnp.int32, (128, 128), 0)
    j = lax.broadcasted_iota(jnp.int32, (128, 128), 1)
    bits = lax.bitwise_and(i, j)
    bits = lax.bitwise_xor(bits, lax.shift_right_logical(bits, 4))
    bits = lax.bitwise_xor(bits, lax.shift_right_logical(bits, 2))
    bits = lax.bitwise_xor(bits, lax.shift_right_logical(bits, 1))
    return (1 - 2 * lax.bitwise_and(bits, 1)).astype(F32)


def sign_table(first):
    i = lax.broadcasted_iota(jnp.int32, (64, 128), 0)
    j = lax.broadcasted_iota(jnp.int32, (64, 128), 1)
    j = j + 128 * lax.shift_right_logical(i, 4) + first
    return (1 - 2 * lax.rem(lax.rem(97 * j, 251), 2)).astype(F32)


def rotate(values, table):
    out = jnp.dot(
        values, table, precision=lax.Precision.HIGHEST, preferred_element_type=F32
    )
    return out * (1.0 / math.sqrt(128.0))


def copy_to(src, dst, send_sem, recv_sem, device):
    return pltpu.make_async_remote_copy(
        src_ref=src,
        dst_ref=dst,
        send_sem=send_sem,
        recv_sem=recv_sem,
        device_id=device,
        device_id_type=pl.DeviceIdType.MESH,
    )


def aligned(index, size):
    return pl.ds(pl.multiple_of(index * size, size), size)


def kernel(
    hidden_in, cot, master_in, adam_m_in, adam_v_in, anchor_in, outer_mom_in, next_in,
    grad_hidden_out, merged_out, anchor_out, mom_out, next_out,
    grad_hidden, results, hidden, state, next_all, cotv, core_send, core_recv,
    part, x_send, x_recv, x_sum, y_send, y_recv, packed, state_in, rot,
    row16, half_in, half_rows, gathered, back_send, back_recv, weights, ahead_send, ahead_out,
    out_sem, next_sem, in_sem, state_sem, cot_sem, nh_ss, nh_rs, core_ss, core_rs,
    x_ss, x_rs, y_ss, y_rs, st_ss, st_rs, rep_ss, rep_rs, back_ss, back_rs,
    agy_ss, agy_rs, half_ss, half_rs, ring_ss, ring_rs, agc_ss, agc_rs, last_ss, last_rs,
):
    rep = lax.axis_index("rep")
    me = lax.axis_index("fsdp")
    z = lax.div(me, 64)
    y = lax.rem(lax.div(me, 8), 8)
    x = lax.rem(lax.div(me, 2), 4)
    c = lax.rem(me, 2)

    def at(zz, yy, xx, cc):
        return {"fsdp": zz * 64 + yy * 8 + xx * 2 + cc}

    group = [
        (1 - z if dz else z, lax.rem(x + dx, 4), 1 - c if dc else c) for dz, dx, dc in OFFSETS
    ]
    place = z * 8 + x * 2 + c
    slice_here = c * 8 + x * 2 + z
    partner = at(z, y, x, 1 - c)
    x_peers = [lax.rem(x + d, 4) for d in range(1, 4)]
    x_from = [lax.rem(x + 4 - d, 4) for d in range(1, 4)]
    y_peers = [lax.rem(y + d, 8) for d in range(1, 8)]

    barrier = pltpu.get_barrier_semaphore()
    peers = [at(zz, y, xx, cc) for zz, xx, cc in group]
    peers += [at(z, yy, x, c) for yy in y_peers]
    peers += [at(1 - z, yy, x, c) for yy in y_peers]
    peers += [{"rep": lax.rem(rep + d, 4)} for d in range(1, 4)]
    for peer in peers:
        pl.semaphore_signal(
            barrier, inc=1, device_id=peer, device_id_type=pl.DeviceIdType.MESH
        )

    sends = []

    def start(copy):
        copy.start()
        sends.append(copy)
        return copy

    halves = (1 - c, c)
    seat = aligned(place, 32)
    loads = [
        pltpu.make_async_copy(hidden_in, hidden, in_sem.at[0]),
        pltpu.make_async_copy(master_in, state.at[0], in_sem.at[1]),
        pltpu.make_async_copy(next_in, next_all.at[seat], in_sem.at[2]),
    ]
    for load in loads:
        load.start()
    chunk_at = [(1 - z if j < 2 else z) * 512 + j % 2 * 256 for j in range(CHUNKS)]
    cot_loads = {}
    for j in range(CHUNKS):
        for h in range(2):
            for s in range(4):
                begin = pl.multiple_of(halves[h] * 4096 + s * 1024 + chunk_at[j], 256)
                load = pltpu.make_async_copy(
                    cot.at[:, pl.ds(begin, 256)],
                    cotv.at[h, j, :, pl.ds(s * 256, 256)],
                    cot_sem.at[h, j, s],
                )
                load.start()
                cot_loads[h, j, s] = load
    late_loads = [
        pltpu.make_async_copy(source, state.at[i + 1], state_sem.at[i])
        for i, source in enumerate((adam_m_in, adam_v_in, anchor_in, outer_mom_in))
    ]
    for load in late_loads:
        load.start()

    order = row_table()
    loads[0].wait()
    turned = lax.dot_general(
        order, hidden[...], (((1,), (1,)), ((), ())), preferred_element_type=F32
    ).astype(BF16)

    y_up, y_down = at(z, y_peers[0], x, c), at(z, y_peers[6], x, c)

    def block_of(distance):
        return aligned(lax.rem(y + 8 + distance, 8), 16)

    half_copies, agc_copies, ring = [], [], {}

    def weights_start():
        loads[1].wait()
        row16[...] = state[0].astype(BF16)
        for i, (zz, xx, cc) in enumerate(group):
            half_copies.append(
                start(
                    copy_to(
                        row16.at[aligned(cc, 32)], half_in.at[place],
                        half_ss.at[i], half_rs.at[i], at(zz, y, xx, cc),
                    )
                )
            )
        half_in[place] = row16[aligned(c, 32), :]

    def to_partner(distance):
        i = len(agc_copies)
        block = block_of(distance)
        agc_copies.append(
            start(
                copy_to(
                    weights.at[1, block], weights.at[0, block],
                    agc_ss.at[i], agc_rs.at[i], partner,
                )
            )
        )

    def weights_step(step):
        if step == 1:
            for copy in half_copies:
                copy.wait_recv()
            half_rows[...] = half_in[...].reshape(512, 128).astype(F32)
            for b in range(32):
                block = half_rows[pl.ds(b, 16, stride=32), :]
                weights[1, block_of(0), b * 128 : (b + 1) * 128] = block.astype(BF16)
        for way, device in ((1, y_up), (-1, y_down)):
            side = 0 if way == 1 else 1
            if step > 1:
                ring[step - 1, way].wait_recv()
            if step == 5:
                continue
            view = weights.at[1, block_of(-way * (step - 1))]
            if step == 4:
                view = view.at[:, pl.ds(side * 2048, 2048)]
            ring[step, way] = start(
                copy_to(view, view, ring_ss.at[side, step - 1], ring_rs.at[side, step - 1], device)
            )
        if step == 1:
            to_partner(0)
        elif step == 5:
            to_partner(4)
        else:
            to_partner(1 - step)
            to_partner(step - 1)

    core_copies = []
    x_copies = {}

    def chunk_to_x(j):
        for s in range(4):
            cot_loads[1, j, s].wait()
        own = jnp.dot(turned, cotv[1, j], preferred_element_type=F32)
        core_copies[j].wait_recv()
        both = own + core_recv[j].astype(F32)
        part[j] = both
        x_send[j] = both.astype(BF16)
        for d in FAR_X:
            x_copies[j, d] = start(
                copy_to(
                    x_send.at[j, :, aligned(x_peers[d], 256)], x_recv.at[j, d],
                    x_ss.at[j, d], x_rs.at[j, d], at(z, y, x_peers[d], c),
                )
            )

    for j in range(CHUNKS):
        for s in range(4):
            cot_loads[0, j, s].wait()
        core_send[j] = jnp.dot(turned, cotv[0, j], preferred_element_type=F32).astype(BF16)
        if j == 0:
            pl.semaphore_wait(barrier, len(peers))
            weights_start()
        core_copies.append(
            start(
                copy_to(
                    core_send.at[j], core_recv.at[j], core_ss.at[j], core_rs.at[j], partner
                )
            )
        )
        if j:
            chunk_to_x(j - 1)
    chunk_to_x(CHUNKS - 1)
    weights_step(1)

    for load in late_loads:
        load.wait()
    for i in range(16):
        for a in range(5):
            packed[i * ARRAYS + 4 * a : i * ARRAYS + 4 * a + 4, :] = state[a, 4 * i : 4 * i + 4, :]
        packed[i * ARRAYS + 20 : i * ARRAYS + 24, :] = jnp.zeros((4, 128), F32)
    state_copies = []
    for i, (zz, xx, cc) in enumerate(group):
        state_copies.append(
            start(
                copy_to(
                    packed.at[aligned(cc * 8 + xx * 2 + zz, ARRAYS)],
                    state_in.at[aligned(place, ARRAYS)],
                    st_ss.at[i], st_rs.at[i], at(zz, y, xx, cc),
                )
            )
        )
    state_in[aligned(place, ARRAYS), :] = packed[aligned(slice_here, ARRAYS), :]

    rs_y = {}
    for j in range(CHUNKS):
        total = part[j, :, aligned(x, 256)]
        for d in range(3):
            x_copies[j, d].wait_recv()
            total = total + x_recv[j, d].astype(F32)
        x_sum[j] = total
        y_send[j] = total.astype(BF16)
        for d in FAR_Y + (0,):
            if d == 0 and j >= 2:
                continue
            yy = lax.rem(y + d, 8)
            rs_y[j, d] = start(
                copy_to(
                    y_send.at[j, aligned(yy, 16)], y_recv.at[j, d],
                    y_ss.at[j, d], y_rs.at[j, d], at(1 - z if j < 2 else z, yy, x, c),
                )
            )
        if j == 0:
            weights_step(2)

    table = hadamard_table()
    signs = sign_table(c * 4096 + x * 1024 + z * 512)
    for copy in state_copies:
        copy.wait_recv()
    master, adam_m, adam_v, anchor, outer_mom = (
        jnp.concatenate(
            [state_in[pl.ds(4 * a + b, 16, stride=ARRAYS), :] for b in range(4)], axis=0
        )
        for a in range(5)
    )
    sums = []
    for k in range(2):
        total = x_sum[2 + k, aligned(y, 16), :]
        for j in (k, 2 + k):
            for d in range(8):
                if (j, d) in rs_y:
                    rs_y[j, d].wait_recv()
                    total = total + y_recv[j, d].astype(F32)
        sums += [total[:, :128], total[:, 128:]]
    gradient = jnp.concatenate(sums, axis=0)

    first = BETA_ONE * adam_m + (1.0 - BETA_ONE) * gradient
    second = BETA_TWO * adam_v + (1.0 - BETA_TWO) * gradient * gradient
    corr_one = 1.0 - BETA_ONE**STEP
    corr_two = 1.0 - BETA_TWO**STEP
    update = first / corr_one / (jnp.sqrt(second / corr_two) + EPS) + DECAY * master
    inner = master - INNER_LR * update
    rot[rep] = rotate((anchor - inner) * signs, table).astype(BF16)
    rep_copies = []
    for d in FAR_X:
        rep_copies.append(
            start(
                copy_to(
                    rot.at[rep], rot.at[rep], rep_ss.at[d], rep_rs.at[d],
                    {"rep": lax.rem(rep + d + 1, 4)},
                )
            )
        )
    weights_step(3)
    loads[2].wait()
    nh_copies = []
    for i, (zz, xx, cc) in enumerate(group):
        nh_copies.append(
            start(
                copy_to(
                    next_all.at[seat], next_all.at[seat],
                    nh_ss.at[i], nh_rs.at[i], at(zz, y, xx, cc),
                )
            )
        )
    for copy in rep_copies:
        copy.wait_recv()
    total = rot[0].astype(F32)
    for r in range(1, 4):
        total = total + rot[r].astype(F32)
    mean_delta = rotate(total, table) * signs * 0.25
    new_momentum = MOMENTUM * outer_mom + mean_delta
    new_anchor = anchor - OUTER_LR * (MOMENTUM * new_momentum + mean_delta)
    merged = ALPHA * inner + (1.0 - ALPHA) * new_anchor
    rows = aligned(y, 16)
    for b in range(4):
        gathered[rows, b * 128 : (b + 1) * 128] = merged[16 * b : 16 * b + 16].astype(BF16)
    agy_copies, stores = [], []
    for q in range(PARTS):
        view = gathered.at[rows, pl.ds(q * WIDE, WIDE)]
        for d in (far - 1 for far in FAR_Y):
            agy_copies.append(
                start(
                    copy_to(
                        view, view, agy_ss.at[q, d], agy_rs.at[q, d], at(z, y_peers[d], x, c)
                    )
                )
            )

    for a, value in enumerate((merged, new_anchor, new_momentum, jnp.zeros((64, 128), F32))):
        for b in range(4):
            back_send[pl.ds(4 * a + b, 16, stride=16), :] = value[16 * b : 16 * b + 16]
    back_copies = []
    for i, (zz, xx, cc) in enumerate(group):
        back_copies.append(
            start(
                copy_to(
                    back_send.at[aligned(zz * 8 + xx * 2 + cc, 16)],
                    back_recv.at[aligned(slice_here, 16)],
                    back_ss.at[i], back_rs.at[i], at(zz, y, xx, cc),
                )
            )
        )
    back_recv[aligned(slice_here, 16), :] = back_send[aligned(place, 16), :]

    def times_weights(h):
        products = jnp.zeros((256, 128), F32)
        for j in range(CHUNKS):
            for s in range(4):
                products = products + lax.dot_general(
                    cotv[h, j, :, s * 256 : (s + 1) * 256],
                    weights[h, :, aligned(s * 4 + lax.div(chunk_at[j], 256), 256)],
                    (((1,), (1,)), ((), ())), preferred_element_type=F32,
                )
        return products

    for copy in nh_copies:
        copy.wait_recv()
    ahead = lax.dot_general(
        next_all[...], order, (((1,), (1,)), ((), ())), preferred_element_type=F32
    ).astype(BF16)
    weights_step(4)

    last = []
    for q in range(PARTS):
        for d in range(7):
            agy_copies[7 * q + d].wait_recv()
        ahead_send[q] = jnp.dot(
            ahead, gathered[:, q * WIDE : (q + 1) * WIDE], preferred_element_type=F32
        ).astype(BF16)
        for i, (zz, xx, cc) in enumerate(group):
            last.append(
                start(
                    copy_to(
                        ahead_send.at[q, aligned(zz * 8 + xx * 2 + cc, 32)],
                        ahead_out.at[slice_here, q],
                        last_ss.at[q, i], last_rs.at[q, i], at(zz, y, xx, cc),
                    )
                )
            )

    weights_step(5)
    products = times_weights(1)
    for copy in agc_copies:
        copy.wait_recv()
    products = products + times_weights(0)
    grad_hidden[...] = jnp.dot(
        products.astype(BF16), order, preferred_element_type=F32
    ).astype(BF16)
    store = pltpu.make_async_copy(grad_hidden, grad_hidden_out, out_sem.at[3])
    store.start()
    stores.append(store)

    for copy in back_copies:
        copy.wait_recv()
    for a, out in enumerate((merged_out, anchor_out, mom_out)):
        for i in range(16):
            results[a, 4 * i : 4 * i + 4, :] = back_recv[16 * i + 4 * a : 16 * i + 4 * a + 4, :]
        store = pltpu.make_async_copy(results.at[a], out, out_sem.at[a])
        store.start()
        stores.append(store)

    sources = [slice_here]
    for dz, dx, dc in OFFSETS:
        sources.append(
            (1 - c if dc else c) * 8 + lax.rem(x + 4 - dx, 4) * 2 + (1 - z if dz else z)
        )
    for q in range(PARTS):
        for i, piece in enumerate(sources):
            view = ahead_send.at[q, seat]
            if i:
                last[15 * q + i - 1].wait_recv()
                view = ahead_out.at[piece, q]
            begin = pl.multiple_of(piece * 512 + q * WIDE, WIDE)
            store = pltpu.make_async_copy(
                view, next_out.at[:, pl.ds(begin, WIDE)], next_sem.at[q, i]
            )
            store.start()
            stores.append(store)
    for store in stores:
        store.wait()
    for copy in sends:
        copy.wait_send()


def store_kernel(*refs):
    sources, outs, held, sems = refs[:5], refs[5:10], refs[10:15], refs[15]
    inward = [pltpu.make_async_copy(a, b, sems.at[0, i]) for i, (a, b) in enumerate(zip(sources, held))]
    outward = [pltpu.make_async_copy(a, b, sems.at[1, i]) for i, (a, b) in enumerate(zip(held, outs))]
    for copy in inward:
        copy.start()
    for come, go in zip(inward, outward):
        come.wait()
        go.start()
    for copy in outward:
        copy.wait()


def shards(hidden, cotangent, master, adam_m, adam_v, anchor, outer_mom, next_hidden):
    hbm = pl.BlockSpec(memory_space=pltpu.HBM)
    dma = lambda *shape: pltpu.SemaphoreType.DMA(shape)
    row = lambda a: a.reshape(64, 128)
    shapes = (
        jax.ShapeDtypeStruct((256, 128), BF16),
        jax.ShapeDtypeStruct((64, 128), F32),
        jax.ShapeDtypeStruct((64, 128), F32),
        jax.ShapeDtypeStruct((64, 128), F32),
        jax.ShapeDtypeStruct((32, 8192), BF16),
    )
    outs = pl.pallas_call(
        kernel,
        out_shape=shapes,
        in_specs=[hbm] * 8,
        out_specs=(hbm,) * 5,
        scratch_shapes=[
            pltpu.VMEM((256, 128), BF16),
            pltpu.VMEM((3, 64, 128), F32),
            pltpu.VMEM((256, 128), BF16),
            pltpu.VMEM((5, 64, 128), F32),
            pltpu.VMEM((512, 128), BF16),
            pltpu.VMEM((2, CHUNKS, 256, 1024), BF16),
            pltpu.VMEM((CHUNKS, 128, 1024), BF16),
            pltpu.VMEM((CHUNKS, 128, 1024), BF16),
            pltpu.VMEM((CHUNKS, 128, 1024), F32),
            pltpu.VMEM((CHUNKS, 128, 1024), BF16),
            pltpu.VMEM((CHUNKS, 3, 128, 256), BF16),
            pltpu.VMEM((CHUNKS, 128, 256), F32),
            pltpu.VMEM((CHUNKS, 128, 256), BF16),
            pltpu.VMEM((CHUNKS, 8, 16, 256), BF16),
            pltpu.VMEM((16 * ARRAYS, 128), F32),
            pltpu.VMEM((16 * ARRAYS, 128), F32),
            pltpu.VMEM((4, 64, 128), BF16),
            pltpu.VMEM((64, 128), BF16),
            pltpu.VMEM((16, 32, 128), BF16),
            pltpu.VMEM((512, 128), F32),
            pltpu.VMEM((128, 512), BF16),
            pltpu.VMEM((256, 128), F32),
            pltpu.VMEM((256, 128), F32),
            pltpu.VMEM((2, 128, 4096), BF16),
            pltpu.VMEM((PARTS, 512, WIDE), BF16),
            pltpu.VMEM((16, PARTS, 32, WIDE), BF16),
            dma(4), dma(PARTS, 16), dma(3), dma(4), dma(2, CHUNKS, 4), dma(15), dma(15),
            dma(CHUNKS), dma(CHUNKS), dma(CHUNKS, 3), dma(CHUNKS, 3),
            dma(CHUNKS, 8), dma(CHUNKS, 8), dma(15), dma(15), dma(3), dma(3),
            dma(15), dma(15), dma(PARTS, 7), dma(PARTS, 7), dma(15), dma(15),
            dma(2, 4), dma(2, 4), dma(8), dma(8), dma(PARTS, 15), dma(PARTS, 15),
        ],
        compiler_params=pltpu.CompilerParams(
            collective_id=0, has_side_effects=True, vmem_limit_bytes=VMEM_BYTES
        ),
        name="sync",
    )(
        hidden[0], cotangent[0], row(master), row(adam_m), row(adam_v),
        row(anchor), row(outer_mom), next_hidden[0],
    )
    outs = pl.pallas_call(
        store_kernel,
        out_shape=shapes,
        in_specs=[hbm] * 5,
        out_specs=(hbm,) * 5,
        scratch_shapes=[pltpu.VMEM(s.shape, s.dtype) for s in shapes] + [dma(2, 5)],
        compiler_params=pltpu.CompilerParams(vmem_limit_bytes=VMEM_BYTES),
        name="store",
    )(*outs)
    grad_hidden, merged, new_anchor, new_momentum, next_out = outs
    return (
        grad_hidden[None],
        merged.reshape(1, 1, 8192),
        new_anchor.reshape(1, 8192),
        new_momentum.reshape(1, 8192),
        next_out[None],
    )


def solution(mesh):
    in_specs = (
        P("rep", "fsdp", None),
        P("rep", "fsdp", None),
        P("rep", "fsdp", None),
        P("rep", "fsdp", None),
        P("rep", "fsdp", None),
        P("fsdp", None),
        P("fsdp", None),
        P("rep", "fsdp", None),
    )
    out_specs = (
        P("rep", "fsdp", None),
        P("rep", "fsdp", None),
        P("fsdp", None),
        P("fsdp", None),
        P("rep", "fsdp", None),
    )
    return jax.shard_map(shards, mesh=mesh, in_specs=in_specs, out_specs=out_specs, check_vma=False)
```
